32 devices in a mesh: grp: 2 (over y), gen: 4 (over z), row: 2 (over x), ch: 2 (over core).
Axes of the slice: x: 2, y: 2, z: 4, core: 2. Of those that a mesh axis runs over, the one named last changes fastest.
Arguments:
- x_center: bfloat16 [24, 24, 112], P(('grp', 'row')), parts along dimension 0, may hold values from -6 to 6
- x_gens: bfloat16 [256, 12, 24, 112], P(('grp', 'gen'), 'row'), parts along dimension 0, may hold values from -0.125 to 0.125
- w_expand: bfloat16 [112, 672], P(None, 'ch'), may hold values from -0.5 to 0.5
- b_expand: float32 [672], P('ch'), may hold values from -3 to 3
- w_depth: float32 [5, 5, 672], P(None, None, 'ch'), may hold values from -1.25 to 1.25
- b_depth: float32 [672], P('ch'), may hold values from -3 to 3
- w_reduce: float32 [672, 28], replicated, may hold values from -0.25 to 0.25
- b_reduce: float32 [28], replicated, may hold values from -6 to 6
- w_excite: float32 [28, 672], P(None, 'ch'), may hold values from -1 to 1
- b_excite: float32 [672], P('ch'), may hold values from -3 to 3
Outputs:
- out_center: float32 [24, 24, 672], P(('grp', 'row'), None, 'ch'), parts along dimension 0
- out_gens: bfloat16 [256, 12, 24, 672], P(('grp', 'gen'), 'row', None, 'ch'), parts along dimension 0
- out_box: float32 [24, 24, 672], P(('grp', 'row'), None, 'ch'), parts along dimension 0
The draws below stay inside these ranges and needn't reach their ends.
There are 2 independent parts, one for each index of `grp`. The reference program is written for one: setup_inputs(seed, part) draws one part's arguments, and reference() takes and returns one part's arrays. A program takes and returns all parts, laid end to end along the dimension named above; an argument that names none is the same for every part. Nothing has to cross between parts.
All inputs are finite; a program needn't handle non-finite values.
Results may differ from the reference program's by a relative error of at most 0.007.
Values may be sent and summed in bfloat16 or wider, within the bound.
A program may use at most 64 MiB of HBM per device.

```python
import jax
import jax.numpy as jnp
from jax import lax

C_IN = 112
C_EXP = 672
C_SE = 28
KSIZE = 5
IMG_W = 24
GEN_DEV = 32
IMG_H = 12
GENS = 128
N_GEN = 4


def draw_x_gens(key, part):
    first_key, second_key = jax.random.split(jax.random.fold_in(key, 11), 2)
    common = jax.random.normal(first_key, (GENS, 1, 1, C_IN))
    rough = jax.random.normal(second_key, (GENS, IMG_H, IMG_W, C_IN))
    factor = 0.01 * jnp.ones((GENS, 1, 1, 1), jnp.float32)
    values = jnp.clip(factor * (common + rough), -0.125, 0.125)
    return values.astype(jnp.bfloat16)


def level_of(key, extent, shards, least, high):
    def one(dim, shards_of):
        draws = jax.random.uniform(jax.random.fold_in(jax.random.fold_in(key, 6), dim), (shards_of,), jnp.float32, least / len(shards), high / len(shards))
        return jnp.repeat(jnp.exp(draws), extent[dim] // shards_of).reshape((-1,) + (1,) * (len(extent) - dim - 1))

    gain = one(*shards[0])
    for cut in shards[1:]:
        gain = gain * one(*cut)
    return gain


def bell_draw(stream_key, shape, spread, most, shards=(), kind=jnp.bfloat16):
    entries = jax.random.normal(stream_key, shape, jnp.float32) * spread
    if len(shards) > 0:
        entries = level_of(stream_key, shape, shards, -0.22, 0.18) * entries
    return jnp.clip(entries, min=-most, max=most).astype(kind)


def setup_inputs(seed: int = 0, part: int = 0) -> dict:
    splits = jax.random.split(jax.random.key(seed), 11)
    own_keys = jax.random.split(jax.random.fold_in(splits[10], part), 11)
    return {
        "x_center": bell_draw(own_keys[0], (IMG_H, IMG_W, C_IN), 1.0, 6.0, ((0, 2),)),
        "x_gens": draw_x_gens(jax.random.fold_in(jax.random.fold_in(splits[10], part), 71), part),
        "w_expand": bell_draw(splits[2], (C_IN, C_EXP), C_IN ** -0.5, 0.5, ((1, 2),)),
        "b_expand": bell_draw(splits[3], (C_EXP,), 0.5, 3.0, ((0, 2),), jnp.float32),
        "w_depth": bell_draw(splits[4], (KSIZE, KSIZE, C_EXP), (KSIZE * KSIZE) ** -0.5, 1.25, ((2, 2),), jnp.float32),
        "b_depth": bell_draw(splits[5], (C_EXP,), 0.5, 3.0, ((0, 2),), jnp.float32),
        "w_reduce": bell_draw(splits[6], (C_EXP, C_SE), C_EXP ** -0.5, 0.25, (), jnp.float32),
        "b_reduce": bell_draw(splits[7], (C_SE,), 1.0, 6.0, (), jnp.float32),
        "w_excite": bell_draw(splits[8], (C_SE, C_EXP), C_SE ** -0.5, 1.0, ((1, 2),), jnp.float32),
        "b_excite": bell_draw(splits[9], (C_EXP,), 0.5, 3.0, ((0, 2),), jnp.float32),
    }


def depthwise(padded, w_depth, row_count, col_count):
    accum_sum = jnp.zeros(padded.shape[:-3] + (row_count, col_count, padded.shape[-1]), jnp.float32)
    for tap_row in range(w_depth.shape[0]):
        for tap_col in range(w_depth.shape[1]):
            window = padded[..., tap_row:tap_row + row_count, tap_col:tap_col + col_count, :]
            accum_sum = accum_sum + window.astype(jnp.float32) * w_depth[tap_row, tap_col]
    return accum_sum


def relax_gate(ex_center, gate_radius):
    low_end = ex_center - gate_radius
    high_end = ex_center + gate_radius
    sig_low = jax.nn.sigmoid(low_end)
    sig_high = jax.nn.sigmoid(high_end)
    slope_val = jnp.minimum(sig_low * (1.0 - sig_low), sig_high * (1.0 - sig_high))
    gate_center = slope_val * ex_center + 0.5 * (sig_high + sig_low - slope_val * (high_end + low_end))
    spread_term = 0.5 * (sig_high - sig_low - slope_val * (high_end - low_end))
    return gate_center, slope_val, spread_term


def reference(x_center, x_gens, w_expand, b_expand, w_depth, b_depth, w_reduce, b_reduce, w_excite, b_excite):
    precise = lax.Precision.HIGHEST
    margin = KSIZE // 2
    padding = [(margin, margin), (margin, margin), (0, 0)]
    exp_center = (jnp.dot(x_center, w_expand, preferred_element_type=jnp.float32) + b_expand).astype(jnp.bfloat16)
    dw_center = depthwise(jnp.pad(exp_center, padding), w_depth, IMG_H, IMG_W) + b_depth
    gen_blocks = x_gens.reshape(N_GEN, GEN_DEV, IMG_H, IMG_W, C_IN)

    def features(gen_block):
        exp_gens = jnp.dot(gen_block, w_expand, preferred_element_type=jnp.float32).astype(jnp.bfloat16)
        return depthwise(jnp.pad(exp_gens, [(0, 0)] + padding), w_depth, IMG_H, IMG_W).astype(jnp.bfloat16)

    def first_pass(running, gen_block):
        dw_gens = features(gen_block).astype(jnp.float32)
        return running + jnp.sum(jnp.abs(dw_gens), axis=0), jnp.sum(dw_gens, axis=(1, 2)) / (IMG_H * IMG_W)

    feat_radius, pool_gens = lax.scan(first_pass, jnp.zeros((IMG_H, IMG_W, C_EXP), jnp.float32), gen_blocks)
    pool_gens = pool_gens.reshape(GENS, C_EXP)
    pool_center = jnp.sum(dw_center, axis=(0, 1)) / (IMG_H * IMG_W)
    sq_center = jnp.dot(pool_center, w_reduce, precision=precise) + b_reduce
    sq_gens = jnp.dot(pool_gens, w_reduce, precision=precise)
    ex_center = jnp.dot(sq_center, w_excite, precision=precise) + b_excite
    ex_gens = jnp.dot(sq_gens, w_excite, precision=precise)
    gate_radius = jnp.sum(jnp.abs(ex_gens), axis=0)
    gate_center, slope_val, spread_term = relax_gate(ex_center, gate_radius)
    gate_gens = slope_val * ex_gens
    gate_total = slope_val * gate_radius + spread_term
    out_center = dw_center * gate_center

    def second_pass(inputs):
        gen_block, gate_block = inputs
        dw_gens = features(gen_block).astype(jnp.float32)
        return (dw_center[None] * gate_block[:, None, None, :] + gate_center * dw_gens).astype(jnp.bfloat16)

    out_gens = lax.map(second_pass, (gen_blocks, gate_gens.reshape(N_GEN, GEN_DEV, C_EXP)))
    out_gens = out_gens.reshape(GENS, IMG_H, IMG_W, C_EXP)
    out_box = jnp.abs(dw_center) * spread_term + feat_radius * gate_total
    return out_center, out_gens, out_box
```

```python
import functools

import jax
import jax.numpy as jnp
from jax import lax
from jax.experimental import pallas as pl
from jax.experimental.pallas import tpu as pltpu
from jax.sharding import PartitionSpec as P

LANES = 128
BLOCK = 4


def conv_rows(src_ref, w_ref, shifted_ref, acc_ref, rows, taps, cols):
    margin = taps // 2
    depth, span, lanes = src_ref.shape
    values = src_ref[...].astype(jnp.float32).reshape(depth * span, lanes)
    col = lax.broadcasted_iota(jnp.int32, (depth * span, lanes), 0) % cols
    for tap_col in range(taps):
        shift = tap_col - margin
        moved = values
        if shift != 0:
            moved = pltpu.roll(values, (-shift) % (depth * span), 0)
            keep = (col + shift >= 0) & (col + shift < cols)
            moved = jnp.where(keep, moved, 0.0)
        shifted_ref[:, :span, :] = moved.astype(jnp.bfloat16).reshape(depth, span, lanes)
        lhs = jnp.concatenate(
            [
                shifted_ref[tap_row : tap_row + rows, :span, :].reshape(rows * span, lanes)
                for tap_row in range(taps)
            ],
            axis=-1,
        )
        part = jnp.dot(lhs, w_ref[tap_col], preferred_element_type=jnp.float32)
        if tap_col == 0:
            acc_ref[: rows * span, :] = part
        else:
            acc_ref[: rows * span, :] += part


def conv_kernel(
    rows, taps, cols, block, chans,
    xg_ref, xc_ref, w_ref, bd_ref,
    dwg_ref, dwc_ref, rad_ref, pg_ref, pc_ref,
    shifted_ref, acc_ref,
):
    step = pl.program_id(0)

    @pl.when(step == 0)
    def _():
        conv_rows(xc_ref, w_ref, shifted_ref, acc_ref, rows, taps, cols)
        total = jnp.zeros((cols, chans), jnp.float32)
        for row in range(rows):
            one = acc_ref[row * 2 * cols : row * 2 * cols + cols, :chans] + bd_ref[...]
            dwc_ref[row] = one
            total = total + one
        pc_ref[...] = jnp.sum(total, axis=0, keepdims=True)
        rad_ref[...] = jnp.zeros_like(rad_ref)

    conv_rows(xg_ref, w_ref, shifted_ref, acc_ref, rows, taps, cols)
    totals = [jnp.zeros((cols, chans), jnp.float32) for _ in range(block)]
    for row in range(rows):
        radius = rad_ref[row]
        for k in range(block):
            start = (row * block + k) * cols
            one = acc_ref[start : start + cols, :chans].astype(jnp.bfloat16)
            dwg_ref[k, row] = one
            wide = one.astype(jnp.float32)
            radius = radius + jnp.abs(wide)
            totals[k] = totals[k] + wide
        rad_ref[row] = radius
    for k in range(block):
        pg_ref[k] = jnp.sum(totals[k], axis=0, keepdims=True)


def conv_call(x_rows, center_rows, weights, b_depth, gens, rows, taps, cols):
    chans = b_depth.shape[0]
    depth = rows + taps - 1
    wide = weights.shape[-1]
    block = BLOCK
    return pl.pallas_call(
        functools.partial(conv_kernel, rows, taps, cols, block, chans),
        grid=(gens // block,),
        in_specs=[
            pl.BlockSpec((depth, block * cols, LANES), lambda i: (0, i, 0)),
            pl.BlockSpec((depth, 2 * cols, LANES), lambda i: (0, 0, 0)),
            pl.BlockSpec(weights.shape, lambda i: (0, 0, 0)),
            pl.BlockSpec((1, chans), lambda i: (0, 0)),
        ],
        out_specs=[
            pl.BlockSpec((block, rows, cols, chans), lambda i: (i, 0, 0, 0)),
            pl.BlockSpec((rows, cols, chans), lambda i: (0, 0, 0)),
            pl.BlockSpec((rows, cols, chans), lambda i: (0, 0, 0)),
            pl.BlockSpec((block, 1, chans), lambda i: (i, 0, 0)),
            pl.BlockSpec((1, chans), lambda i: (0, 0)),
        ],
        out_shape=[
            jax.ShapeDtypeStruct((gens, rows, cols, chans), jnp.bfloat16),
            jax.ShapeDtypeStruct((rows, cols, chans), jnp.float32),
            jax.ShapeDtypeStruct((rows, cols, chans), jnp.float32),
            jax.ShapeDtypeStruct((gens, 1, chans), jnp.float32),
            jax.ShapeDtypeStruct((1, chans), jnp.float32),
        ],
        scratch_shapes=[
            pltpu.VMEM((depth, block * cols, LANES), jnp.bfloat16),
            pltpu.VMEM((rows * block * cols, wide), jnp.float32),
        ],
        compiler_params=pltpu.CompilerParams(
            dimension_semantics=("arbitrary",), vmem_limit_bytes=40 << 20
        ),
        cost_estimate=pl.CostEstimate(
            flops=2 * gens * rows * cols * taps * taps * LANES * wide,
            bytes_accessed=10 << 20,
            transcendentals=0,
        ),
    )(x_rows, center_rows, weights, b_depth[None])


def relax_gate(ex_center, gate_radius):
    low_end = ex_center - gate_radius
    high_end = ex_center + gate_radius
    sig_low = jax.nn.sigmoid(low_end)
    sig_high = jax.nn.sigmoid(high_end)
    slope_val = jnp.minimum(sig_low * (1.0 - sig_low), sig_high * (1.0 - sig_high))
    gate_center = slope_val * ex_center + 0.5 * (
        sig_high + sig_low - slope_val * (high_end + low_end)
    )
    spread_term = 0.5 * (sig_high - sig_low - slope_val * (high_end - low_end))
    return (gate_center, slope_val, spread_term)


def merged_weights(w_expand, b_expand, w_depth):
    taps = w_depth.shape[0]
    c_in, chans = w_expand.shape
    wide = -(-chans // LANES) * LANES
    bias = b_expand.astype(jnp.bfloat16)
    rest = (b_expand - bias.astype(jnp.float32)).astype(jnp.bfloat16)
    mixed = jnp.concatenate([w_expand, bias[None], rest[None]], axis=0)
    mixed = jnp.pad(mixed, ((0, LANES - c_in - 2), (0, wide - chans))).astype(jnp.float32)
    depth = jnp.pad(w_depth, ((0, 0), (0, 0), (0, wide - chans))).transpose(1, 0, 2)
    merged = (depth[:, :, None, :] * mixed[None, None]).astype(jnp.bfloat16)
    return merged.reshape(taps, taps * LANES, wide)


def with_halo(rows_first, axis, margin):
    count = lax.axis_size(axis)
    ends = count - 1
    head = rows_first[:margin]
    tail = rows_first[-margin:]
    above = lax.ppermute(tail, axis, [(i, i + 1) for i in range(ends)])
    below = lax.ppermute(head, axis, [(i + 1, i) for i in range(ends)])
    return above, below


def on_device(
    x_center, x_gens, w_expand, b_expand, w_depth, b_depth, w_reduce, b_reduce, w_excite, b_excite
):
    precise = lax.Precision.HIGHEST
    gens, rows, cols, c_in = x_gens.shape
    chans = w_expand.shape[1]
    taps = w_depth.shape[0]
    margin = taps // 2
    cells = rows * lax.axis_size("row") * cols
    weights = merged_weights(w_expand, b_expand, w_depth)
    flat = x_gens.transpose(1, 0, 2, 3).reshape(rows, gens * cols, c_in)
    ones = jnp.ones((rows, cols, 2), jnp.bfloat16)
    center = jnp.concatenate([x_center, ones], axis=-1)
    above, below = with_halo(flat, "row", margin)
    above_c, below_c = with_halo(center, "row", margin)
    x_rows = jnp.pad(
        jnp.concatenate([above, flat, below], axis=0), ((0, 0), (0, 0), (0, LANES - c_in))
    )
    center_rows = jnp.pad(
        jnp.concatenate([above_c, center, below_c], axis=0),
        ((0, 0), (0, cols), (0, LANES - c_in - 2)),
    )
    dw_gens, dw_center, local_radius, sum_gens, sum_center = conv_call(
        x_rows, center_rows, weights, b_depth, gens, rows, taps, cols
    )
    feat_radius = lax.psum(local_radius.astype(jnp.bfloat16), "gen").astype(jnp.float32)
    pooled = jnp.concatenate([sum_gens[:, 0], sum_center], axis=0) * (1.0 / cells)
    own = lax.dynamic_slice_in_dim(w_reduce, lax.axis_index("ch") * chans, chans, 0)
    squeezed = lax.psum(jnp.dot(pooled, own, precision=precise), ("row", "ch"))
    ex_all = jnp.dot(squeezed, w_excite, precision=precise)
    ex_gens = ex_all[:gens]
    ex_center = ex_all[gens] + jnp.dot(b_reduce, w_excite, precision=precise) + b_excite
    gate_radius = lax.psum(jnp.sum(jnp.abs(ex_gens), axis=0), "gen")
    gate_center, slope_val, spread_term = relax_gate(ex_center, gate_radius)
    gate_gens = slope_val * ex_gens
    gate_total = slope_val * gate_radius + spread_term
    out_center = dw_center * gate_center
    out_gens = (
        dw_center[None] * gate_gens[:, None, None, :] + gate_center * dw_gens.astype(jnp.float32)
    ).astype(jnp.bfloat16)
    out_box = jnp.abs(dw_center) * spread_term + feat_radius * gate_total
    return (out_center, out_gens, out_box)


def solution(mesh):
    in_specs = (
        P(("grp", "row"), None, None),
        P(("grp", "gen"), "row", None, None),
        P(None, "ch"),
        P("ch"),
        P(None, None, "ch"),
        P("ch"),
        P(),
        P(),
        P(None, "ch"),
        P("ch"),
    )
    out_specs = (
        P(("grp", "row"), None, "ch"),
        P(("grp", "gen"), "row", None, "ch"),
        P(("grp", "row"), None, "ch"),
    )
    return jax.shard_map(
        on_device, mesh=mesh, in_specs=in_specs, out_specs=out_specs, check_vma=False
    )
```

```python
import functools

import jax
import jax.numpy as jnp
from jax import lax
from jax.experimental import pallas as pl
from jax.experimental.pallas import tpu as pltpu
from jax.sharding import PartitionSpec as P

MESH = pl.DeviceIdType.MESH
LANES = 128
BLOCK = 4


def conv_rows(src_ref, w_ref, shifted_ref, acc_ref, rows, taps, cols):
    margin = taps // 2
    depth, span, lanes = src_ref.shape
    values = src_ref[...].astype(jnp.float32).reshape(depth * span, lanes)
    col = lax.broadcasted_iota(jnp.int32, (depth * span, lanes), 0) % cols
    for tap_col in range(taps):
        shift = tap_col - margin
        moved = values
        if shift != 0:
            moved = pltpu.roll(values, (-shift) % (depth * span), 0)
            keep = (col + shift >= 0) & (col + shift < cols)
            moved = jnp.where(keep, moved, 0.0)
        shifted_ref[:, :span, :] = moved.astype(jnp.bfloat16).reshape(depth, span, lanes)
        lhs = jnp.concatenate(
            [
                shifted_ref[tap_row : tap_row + rows, :span, :].reshape(rows * span, lanes)
                for tap_row in range(taps)
            ],
            axis=-1,
        )
        part = jnp.dot(lhs, w_ref[tap_col], preferred_element_type=jnp.float32)
        if tap_col == 0:
            acc_ref[: rows * span, :] = part
        else:
            acc_ref[: rows * span, :] += part


def conv_kernel(
    rows, taps, cols, block, chans,
    xg_ref, xc_ref, w_ref, bd_ref,
    dwg_ref, dwc_ref, rad_ref, pg_ref, pc_ref,
    shifted_ref, acc_ref,
):
    step = pl.program_id(0)

    @pl.when(step == 0)
    def _():
        conv_rows(xc_ref, w_ref, shifted_ref, acc_ref, rows, taps, cols)
        total = jnp.zeros((cols, chans), jnp.float32)
        for row in range(rows):
            one = acc_ref[row * 2 * cols : row * 2 * cols + cols, :chans] + bd_ref[...]
            dwc_ref[row] = one
            total = total + one
        pc_ref[...] = jnp.sum(total, axis=0, keepdims=True)
        rad_ref[...] = jnp.zeros_like(rad_ref)

    conv_rows(xg_ref, w_ref, shifted_ref, acc_ref, rows, taps, cols)
    totals = [jnp.zeros((cols, chans), jnp.float32) for _ in range(block)]
    for row in range(rows):
        radius = rad_ref[row]
        for k in range(block):
            start = (row * block + k) * cols
            one = acc_ref[start : start + cols, :chans].astype(jnp.bfloat16)
            dwg_ref[k, row] = one
            wide = one.astype(jnp.float32)
            radius = radius + jnp.abs(wide)
            totals[k] = totals[k] + wide
        rad_ref[row] = radius
    for k in range(block):
        pg_ref[k] = jnp.sum(totals[k], axis=0, keepdims=True)


def conv_call(x_rows, center_rows, weights, b_depth, gens, rows, taps, cols):
    chans = b_depth.shape[0]
    depth = rows + taps - 1
    wide = weights.shape[-1]
    block = BLOCK
    return pl.pallas_call(
        functools.partial(conv_kernel, rows, taps, cols, block, chans),
        grid=(gens // block,),
        in_specs=[
            pl.BlockSpec((depth, block * cols, LANES), lambda i: (0, i, 0)),
            pl.BlockSpec((depth, 2 * cols, LANES), lambda i: (0, 0, 0)),
            pl.BlockSpec(weights.shape, lambda i: (0, 0, 0)),
            pl.BlockSpec((1, chans), lambda i: (0, 0)),
        ],
        out_specs=[
            pl.BlockSpec((block, rows, cols, chans), lambda i: (i, 0, 0, 0)),
            pl.BlockSpec((rows, cols, chans), lambda i: (0, 0, 0)),
            pl.BlockSpec((rows, cols, chans), lambda i: (0, 0, 0)),
            pl.BlockSpec((block, 1, chans), lambda i: (i, 0, 0)),
            pl.BlockSpec((1, chans), lambda i: (0, 0)),
        ],
        out_shape=[
            jax.ShapeDtypeStruct((gens, rows, cols, chans), jnp.bfloat16),
            jax.ShapeDtypeStruct((rows, cols, chans), jnp.float32),
            jax.ShapeDtypeStruct((rows, cols, chans), jnp.float32),
            jax.ShapeDtypeStruct((gens, 1, chans), jnp.float32),
            jax.ShapeDtypeStruct((1, chans), jnp.float32),
        ],
        scratch_shapes=[
            pltpu.VMEM((depth, block * cols, LANES), jnp.bfloat16),
            pltpu.VMEM((rows * block * cols, wide), jnp.float32),
        ],
        compiler_params=pltpu.CompilerParams(
            dimension_semantics=("arbitrary",), vmem_limit_bytes=40 << 20
        ),
        cost_estimate=pl.CostEstimate(
            flops=2 * gens * rows * cols * taps * taps * LANES * wide,
            bytes_accessed=10 << 20,
            transcendentals=0,
        ),
    )(x_rows, center_rows, weights, b_depth[None])


def relax_gate(ex_center, gate_radius):
    low_end = ex_center - gate_radius
    high_end = ex_center + gate_radius
    sig_low = jax.nn.sigmoid(low_end)
    sig_high = jax.nn.sigmoid(high_end)
    slope_val = jnp.minimum(sig_low * (1.0 - sig_low), sig_high * (1.0 - sig_high))
    gate_center = slope_val * ex_center + 0.5 * (
        sig_high + sig_low - slope_val * (high_end + low_end)
    )
    spread_term = 0.5 * (sig_high - sig_low - slope_val * (high_end - low_end))
    return (gate_center, slope_val, spread_term)


def exchange_kernel(
    gens, rows, cols, count_gen, count_row, count_ch, per,
    rad_ref, sg_ref, sc_ref, wr_ref, br_ref, we_ref, be_ref,
    gates_ref, stats_ref, feat_ref,
    send_rad, recv_rad, full_rad, squeeze, gate,
    rs_send, rs_recv, ag_send, ag_recv, sq_send, sq_recv, gt_send, gt_recv,
):
    my_gen = lax.axis_index("gen")
    my_row = lax.axis_index("row")
    my_ch = lax.axis_index("ch")
    chans = stats_ref.shape[-1]
    cells = rows * cols * count_row
    gen_peers = [(off, {"gen": lax.rem(my_gen + off, count_gen)}) for off in range(1, count_gen)]
    side_peers = []
    for off_row in range(count_row):
        for off_ch in range(count_ch):
            if off_row or off_ch:
                place = {
                    "row": lax.rem(my_row + off_row, count_row),
                    "ch": lax.rem(my_ch + off_ch, count_ch),
                }
                side_peers.append((off_row * count_ch + off_ch, place))
    barrier = pltpu.get_barrier_semaphore()
    for _, place in gen_peers + side_peers:
        pl.semaphore_signal(barrier, inc=1, device_id=place, device_id_type=MESH)

    pooled = jnp.concatenate(
        [sg_ref[...], sc_ref[...], jnp.zeros((7, chans), jnp.float32)], axis=0
    ) * (1.0 / cells)
    part = jnp.dot(
        pooled, wr_ref[...], precision=lax.Precision.HIGHEST, preferred_element_type=jnp.float32
    )
    mine = my_row * count_ch + my_ch
    squeeze[mine] = part
    tiles = rows * cols // 8
    send_rad[:tiles] = rad_ref[...].reshape(tiles, 8, chans).astype(jnp.bfloat16)
    if count_gen * per > tiles:
        send_rad[tiles:] = jnp.zeros((count_gen * per - tiles, 8, chans), jnp.bfloat16)
    recv_rad[my_gen] = send_rad[pl.ds(my_gen * per, per)]

    pl.semaphore_wait(barrier, len(gen_peers) + len(side_peers))

    def remote(src, dst, send_sem, recv_sem, place):
        return pltpu.make_async_remote_copy(
            src_ref=src, dst_ref=dst, send_sem=send_sem, recv_sem=recv_sem,
            device_id=place, device_id_type=MESH,
        )

    sq_copies = [
        remote(squeeze.at[mine], squeeze.at[mine], sq_send.at[off], sq_recv.at[off], place)
        for off, place in side_peers
    ]
    rs_copies = [
        remote(
            send_rad.at[pl.ds(place["gen"] * per, per)], recv_rad.at[my_gen],
            rs_send.at[off], rs_recv.at[off], place,
        )
        for off, place in gen_peers
    ]
    for copy in sq_copies + rs_copies:
        copy.start()
    for copy in sq_copies:
        copy.wait()
    total = squeeze[0]
    for slot in range(1, count_row * count_ch):
        total = total + squeeze[slot]
    row_of = lax.broadcasted_iota(jnp.int32, total.shape, 0)
    total = total + jnp.where(row_of == gens, br_ref[...], 0.0)
    ex_all = jnp.dot(
        total, we_ref[...], precision=lax.Precision.HIGHEST, preferred_element_type=jnp.float32
    )
    ex_gens = ex_all[:gens]
    ex_center = ex_all[gens : gens + 1] + be_ref[...]
    gate[my_gen] = jnp.sum(jnp.abs(ex_gens), axis=0, keepdims=True)
    gt_copies = [
        remote(gate.at[my_gen], gate.at[my_gen], gt_send.at[off], gt_recv.at[off], place)
        for off, place in gen_peers
    ]
    for copy in gt_copies:
        copy.start()

    for copy in rs_copies:
        copy.wait()
    chunk = recv_rad[0].astype(jnp.float32)
    for slot in range(1, count_gen):
        chunk = chunk + recv_rad[slot].astype(jnp.float32)
    own = pl.ds(my_gen * per, per)
    full_rad[own] = chunk.astype(jnp.bfloat16)
    ag_copies = [
        remote(full_rad.at[own], full_rad.at[own], ag_send.at[off], ag_recv.at[off], place)
        for off, place in gen_peers
    ]
    for copy in ag_copies:
        copy.start()

    for copy in gt_copies:
        copy.wait()
    gate_radius = gate[0]
    for slot in range(1, count_gen):
        gate_radius = gate_radius + gate[slot]
    gate_center, slope_val, spread_term = relax_gate(ex_center, gate_radius)
    gates_ref[...] = slope_val * ex_gens
    gate_total = slope_val * gate_radius + spread_term
    stats_ref[0:1] = gate_center
    stats_ref[1:2] = spread_term
    stats_ref[2:3] = gate_total
    for copy in ag_copies:
        copy.wait()
    feat_ref[...] = full_rad[:tiles].astype(jnp.float32).reshape(rows, cols, chans)


def exchange_call(mesh, radius, sum_gens, sum_center, w_own, b_reduce, w_excite, b_excite):
    rows, cols, chans = radius.shape
    gens = sum_gens.shape[0]
    count_gen, count_row, count_ch = mesh["gen"], mesh["row"], mesh["ch"]
    per = -(-(rows * cols // 8) // count_gen)
    units = w_own.shape[1]
    vmem = pl.BlockSpec(memory_space=pltpu.VMEM)
    side = count_row * count_ch
    dma = pltpu.SemaphoreType.DMA
    return pl.pallas_call(
        functools.partial(exchange_kernel, gens, rows, cols, count_gen, count_row, count_ch, per),
        in_specs=[vmem] * 7,
        out_specs=[vmem] * 3,
        out_shape=[
            jax.ShapeDtypeStruct((gens, chans), jnp.float32),
            jax.ShapeDtypeStruct((3, chans), jnp.float32),
            jax.ShapeDtypeStruct((rows, cols, chans), jnp.float32),
        ],
        scratch_shapes=[
            pltpu.VMEM((count_gen * per, 8, chans), jnp.bfloat16),
            pltpu.VMEM((count_gen, per, 8, chans), jnp.bfloat16),
            pltpu.VMEM((count_gen * per, 8, chans), jnp.bfloat16),
            pltpu.VMEM((side, gens + 8, units), jnp.float32),
            pltpu.VMEM((count_gen, 1, chans), jnp.float32),
            dma((count_gen,)), dma((count_gen,)), dma((count_gen,)), dma((count_gen,)),
            dma((side,)), dma((side,)), dma((count_gen,)), dma((count_gen,)),
        ],
        compiler_params=pltpu.CompilerParams(
            collective_id=1, has_side_effects=True, vmem_limit_bytes=32 << 20
        ),
    )(radius, sum_gens, sum_center, w_own, b_reduce[None], w_excite, b_excite[None])


def final_kernel(block, dwg_ref, gates_ref, dwc_ref, feat_ref, stats_ref, oc_ref, og_ref, ob_ref):
    center = dwc_ref[...]
    gate_center = stats_ref[0:1]

    @pl.when(pl.program_id(0) == 0)
    def _():
        oc_ref[...] = center * gate_center
        ob_ref[...] = jnp.abs(center) * stats_ref[1:2] + feat_ref[...] * stats_ref[2:3]

    for k in range(block):
        og_ref[k] = (
            center * gates_ref[k] + gate_center * dwg_ref[k].astype(jnp.float32)
        ).astype(jnp.bfloat16)


def final_call(dw_gens, gates, dw_center, feat, stats):
    gens, rows, cols, chans = dw_gens.shape
    block = 8
    whole = pl.BlockSpec((rows, cols, chans), lambda i: (0, 0, 0))
    big = pl.BlockSpec((block, rows, cols, chans), lambda i: (i, 0, 0, 0))
    return pl.pallas_call(
        functools.partial(final_kernel, block),
        grid=(gens // block,),
        in_specs=[
            big,
            pl.BlockSpec((block, 1, chans), lambda i: (i, 0, 0)),
            whole,
            whole,
            pl.BlockSpec((3, chans), lambda i: (0, 0)),
        ],
        out_specs=[whole, big, whole],
        out_shape=[
            jax.ShapeDtypeStruct((rows, cols, chans), jnp.float32),
            jax.ShapeDtypeStruct(dw_gens.shape, jnp.bfloat16),
            jax.ShapeDtypeStruct((rows, cols, chans), jnp.float32),
        ],
        compiler_params=pltpu.CompilerParams(
            dimension_semantics=("arbitrary",), vmem_limit_bytes=32 << 20
        ),
    )(dw_gens, gates[:, None], dw_center, feat, stats)


def merged_weights(w_expand, b_expand, w_depth):
    taps = w_depth.shape[0]
    c_in, chans = w_expand.shape
    wide = -(-chans // LANES) * LANES
    bias = b_expand.astype(jnp.bfloat16)
    rest = (b_expand - bias.astype(jnp.float32)).astype(jnp.bfloat16)
    mixed = jnp.concatenate([w_expand, bias[None], rest[None]], axis=0)
    mixed = jnp.pad(mixed, ((0, LANES - c_in - 2), (0, wide - chans))).astype(jnp.float32)
    depth = jnp.pad(w_depth, ((0, 0), (0, 0), (0, wide - chans))).transpose(1, 0, 2)
    merged = (depth[:, :, None, :] * mixed[None, None]).astype(jnp.bfloat16)
    return merged.reshape(taps, taps * LANES, wide)


def with_halo(rows_first, axis, margin):
    count = lax.axis_size(axis)
    ends = count - 1
    head = rows_first[:margin]
    tail = rows_first[-margin:]
    above = lax.ppermute(tail, axis, [(i, i + 1) for i in range(ends)])
    below = lax.ppermute(head, axis, [(i + 1, i) for i in range(ends)])
    return above, below


def on_device(
    shape, x_center, x_gens, w_expand, b_expand, w_depth, b_depth, w_reduce, b_reduce, w_excite, b_excite
):
    gens, rows, cols, c_in = x_gens.shape
    chans = w_expand.shape[1]
    taps = w_depth.shape[0]
    margin = taps // 2
    weights = merged_weights(w_expand, b_expand, w_depth)
    flat = x_gens.transpose(1, 0, 2, 3).reshape(rows, gens * cols, c_in)
    ones = jnp.ones((rows, cols, 2), jnp.bfloat16)
    center = jnp.concatenate([x_center, ones], axis=-1)
    above, below = with_halo(flat, "row", margin)
    above_c, below_c = with_halo(center, "row", margin)
    x_rows = jnp.pad(
        jnp.concatenate([above, flat, below], axis=0), ((0, 0), (0, 0), (0, LANES - c_in))
    )
    center_rows = jnp.pad(
        jnp.concatenate([above_c, center, below_c], axis=0),
        ((0, 0), (0, cols), (0, LANES - c_in - 2)),
    )
    dw_gens, dw_center, local_radius, sum_gens, sum_center = conv_call(
        x_rows, center_rows, weights, b_depth, gens, rows, taps, cols
    )
    own = lax.dynamic_slice_in_dim(w_reduce, lax.axis_index("ch") * chans, chans, 0)
    spare = LANES - own.shape[1]
    gates, stats, feat = exchange_call(
        shape,
        local_radius,
        sum_gens[:, 0],
        sum_center,
        jnp.pad(own, ((0, 0), (0, spare))),
        jnp.pad(b_reduce, (0, spare)),
        jnp.pad(w_excite, ((0, spare), (0, 0))),
        b_excite,
    )
    return final_call(dw_gens, gates, dw_center, feat, stats)


def solution(mesh):
    in_specs = (
        P(("grp", "row"), None, None),
        P(("grp", "gen"), "row", None, None),
        P(None, "ch"),
        P("ch"),
        P(None, None, "ch"),
        P("ch"),
        P(),
        P(),
        P(None, "ch"),
        P("ch"),
    )
    out_specs = (
        P(("grp", "row"), None, "ch"),
        P(("grp", "gen"), "row", None, "ch"),
        P(("grp", "row"), None, "ch"),
    )
    return jax.shard_map(
        functools.partial(on_device, dict(mesh.shape)), mesh=mesh, in_specs=in_specs, out_specs=out_specs, check_vma=False
    )
```

```python
import functools

import jax
import jax.numpy as jnp
from jax import lax
from jax.experimental import pallas as pl
from jax.experimental.pallas import tpu as pltpu
from jax.sharding import PartitionSpec as P

MESH = pl.DeviceIdType.MESH
LANES = 128
BLOCK = 4


def conv_rows(src_ref, w_ref, shifted_ref, acc_ref, rows, taps, cols):
    margin = taps // 2
    depth, span, lanes = src_ref.shape
    values = src_ref[...].astype(jnp.float32).reshape(depth * span, lanes)
    col = lax.broadcasted_iota(jnp.int32, (depth * span, lanes), 0) % cols
    for tap_col in range(taps):
        shift = tap_col - margin
        moved = values
        if shift != 0:
            moved = pltpu.roll(values, (-shift) % (depth * span), 0)
            keep = (col + shift >= 0) & (col + shift < cols)
            moved = jnp.where(keep, moved, 0.0)
        shifted_ref[:, :span, :] = moved.astype(jnp.bfloat16).reshape(depth, span, lanes)
        lhs = jnp.concatenate(
            [
                shifted_ref[tap_row : tap_row + rows, :span, :].reshape(rows * span, lanes)
                for tap_row in range(taps)
            ],
            axis=-1,
        )
        part = jnp.dot(lhs, w_ref[tap_col], preferred_element_type=jnp.float32)
        if tap_col == 0:
            acc_ref[: rows * span, :] = part
        else:
            acc_ref[: rows * span, :] += part


def conv_kernel(
    rows, taps, cols, block, chans,
    xg_ref, xc_ref, w_ref, bd_ref,
    dwg_ref, dwc_ref, rad_ref, pg_ref, pc_ref,
    shifted_ref, acc_ref,
):
    step = pl.program_id(0)

    @pl.when(step == 0)
    def _():
        conv_rows(xc_ref, w_ref, shifted_ref, acc_ref, rows, taps, cols)
        total = jnp.zeros((cols, chans), jnp.float32)
        for row in range(rows):
            one = acc_ref[row * 2 * cols : row * 2 * cols + cols, :chans] + bd_ref[0:1]
            dwc_ref[row] = one
            total = total + one
        pc_ref[...] = jnp.sum(total, axis=0, keepdims=True)
        rad_ref[...] = jnp.zeros_like(rad_ref)

    conv_rows(xg_ref, w_ref, shifted_ref, acc_ref, rows, taps, cols)
    totals = [jnp.zeros((cols, chans), jnp.float32) for _ in range(block)]
    for row in range(rows):
        radius = rad_ref[row]
        for k in range(block):
            start = (row * block + k) * cols
            one = acc_ref[start : start + cols, :chans].astype(jnp.bfloat16)
            dwg_ref[k, row] = one
            wide = one.astype(jnp.float32)
            radius = radius + jnp.abs(wide)
            totals[k] = totals[k] + wide
        rad_ref[row] = radius
    for k in range(block):
        pg_ref[k] = jnp.sum(totals[k], axis=0, keepdims=True)


def conv_call(x_rows, weights, vectors, gens, rows, taps, cols):
    chans = vectors.shape[1]
    depth = rows + taps - 1
    wide = weights.shape[-1]
    block = BLOCK
    return pl.pallas_call(
        functools.partial(conv_kernel, rows, taps, cols, block, chans),
        grid=(gens // block,),
        in_specs=[
            pl.BlockSpec((depth, block * cols, LANES), lambda i: (0, i, 0)),
            pl.BlockSpec((depth, 2 * cols, LANES), lambda i: (0, gens // 2, 0)),
            pl.BlockSpec(weights.shape, lambda i: (0, 0, 0)),
            pl.BlockSpec(vectors.shape, lambda i: (0, 0)),
        ],
        out_specs=[
            pl.BlockSpec((block, rows, cols, chans), lambda i: (i, 0, 0, 0)),
            pl.BlockSpec((rows, cols, chans), lambda i: (0, 0, 0)),
            pl.BlockSpec((rows, cols, chans), lambda i: (0, 0, 0)),
            pl.BlockSpec((block, 1, chans), lambda i: (i, 0, 0)),
            pl.BlockSpec((1, chans), lambda i: (0, 0)),
        ],
        out_shape=[
            jax.ShapeDtypeStruct((gens, rows, cols, chans), jnp.bfloat16),
            jax.ShapeDtypeStruct((rows, cols, chans), jnp.float32),
            jax.ShapeDtypeStruct((rows, cols, chans), jnp.float32),
            jax.ShapeDtypeStruct((gens, 1, chans), jnp.float32),
            jax.ShapeDtypeStruct((1, chans), jnp.float32),
        ],
        scratch_shapes=[
            pltpu.VMEM((depth, block * cols, LANES), jnp.bfloat16),
            pltpu.VMEM((rows * block * cols, wide), jnp.float32),
        ],
        compiler_params=pltpu.CompilerParams(
            dimension_semantics=("arbitrary",), vmem_limit_bytes=40 << 20
        ),
        cost_estimate=pl.CostEstimate(
            flops=2 * gens * rows * cols * taps * taps * LANES * wide,
            bytes_accessed=10 << 20,
            transcendentals=0,
        ),
    )(x_rows, x_rows, weights, vectors)


def relax_gate(ex_center, gate_radius):
    low_end = ex_center - gate_radius
    high_end = ex_center + gate_radius
    sig_low = jax.nn.sigmoid(low_end)
    sig_high = jax.nn.sigmoid(high_end)
    slope_val = jnp.minimum(sig_low * (1.0 - sig_low), sig_high * (1.0 - sig_high))
    gate_center = slope_val * ex_center + 0.5 * (
        sig_high + sig_low - slope_val * (high_end + low_end)
    )
    spread_term = 0.5 * (sig_high - sig_low - slope_val * (high_end - low_end))
    return (gate_center, slope_val, spread_term)


def exchange_kernel(
    gens, rows, cols, count_gen, count_row, count_ch, per,
    rad_ref, sg_ref, sc_ref, wr_ref, we_ref, vec_ref,
    gates_ref, stats_ref, feat_ref,
    send_rad, recv_rad, full_rad, squeeze, gate,
    rs_send, rs_recv, ag_send, ag_recv, sq_send, sq_recv, gt_send, gt_recv,
):
    my_gen = lax.axis_index("gen")
    my_row = lax.axis_index("row")
    my_ch = lax.axis_index("ch")
    chans = stats_ref.shape[-1]
    units = we_ref.shape[0]
    cells = rows * cols * count_row
    gen_peers = [(off, {"gen": lax.rem(my_gen + off, count_gen)}) for off in range(1, count_gen)]
    side_peers = []
    for off_row in range(count_row):
        for off_ch in range(count_ch):
            if off_row or off_ch:
                place = {
                    "row": lax.rem(my_row + off_row, count_row),
                    "ch": lax.rem(my_ch + off_ch, count_ch),
                }
                side_peers.append((off_row * count_ch + off_ch, place))
    barrier = pltpu.get_barrier_semaphore()
    for _, place in gen_peers + side_peers:
        pl.semaphore_signal(barrier, inc=1, device_id=place, device_id_type=MESH)

    pooled = jnp.concatenate(
        [sg_ref[...][:, 0], sc_ref[...], jnp.zeros((7, chans), jnp.float32)], axis=0
    ) * (1.0 / cells)
    part = jnp.dot(
        pooled, wr_ref[pl.ds(pl.multiple_of(my_ch * chans, 8), chans)],
        precision=lax.Precision.HIGHEST,
        preferred_element_type=jnp.float32,
    )
    mine = my_row * count_ch + my_ch
    squeeze[mine] = part
    tiles = rows * cols // 8
    send_rad[:tiles] = rad_ref[...].reshape(tiles, 8, chans).astype(jnp.bfloat16)
    if count_gen * per > tiles:
        send_rad[tiles:] = jnp.zeros((count_gen * per - tiles, 8, chans), jnp.bfloat16)
    recv_rad[my_gen] = send_rad[pl.ds(my_gen * per, per)]

    pl.semaphore_wait(barrier, len(gen_peers) + len(side_peers))

    def remote(src, dst, send_sem, recv_sem, place):
        return pltpu.make_async_remote_copy(
            src_ref=src, dst_ref=dst, send_sem=send_sem, recv_sem=recv_sem,
            device_id=place, device_id_type=MESH,
        )

    sq_copies = [
        remote(squeeze.at[mine], squeeze.at[mine], sq_send.at[off], sq_recv.at[off], place)
        for off, place in side_peers
    ]
    rs_copies = [
        remote(
            send_rad.at[pl.ds(place["gen"] * per, per)], recv_rad.at[my_gen],
            rs_send.at[off], rs_recv.at[off], place,
        )
        for off, place in gen_peers
    ]
    for copy in sq_copies + rs_copies:
        copy.start()
    for copy in sq_copies:
        copy.wait()
    total = squeeze[0]
    for slot in range(1, count_row * count_ch):
        total = total + squeeze[slot]
    row_of = lax.broadcasted_iota(jnp.int32, total.shape, 0)
    total = total + jnp.where(row_of == gens, vec_ref[2:3, :units], 0.0)
    ex_all = jnp.dot(
        total, we_ref[...], precision=lax.Precision.HIGHEST, preferred_element_type=jnp.float32
    )
    ex_gens = ex_all[:gens]
    ex_center = ex_all[gens : gens + 1] + vec_ref[1:2]
    gate[my_gen] = jnp.sum(jnp.abs(ex_gens), axis=0, keepdims=True)
    gt_copies = [
        remote(gate.at[my_gen], gate.at[my_gen], gt_send.at[off], gt_recv.at[off], place)
        for off, place in gen_peers
    ]
    for copy in gt_copies:
        copy.start()

    for copy in rs_copies:
        copy.wait()
    chunk = recv_rad[0].astype(jnp.float32)
    for slot in range(1, count_gen):
        chunk = chunk + recv_rad[slot].astype(jnp.float32)
    own = pl.ds(my_gen * per, per)
    full_rad[own] = chunk.astype(jnp.bfloat16)
    ag_copies = [
        remote(full_rad.at[own], full_rad.at[own], ag_send.at[off], ag_recv.at[off], place)
        for off, place in gen_peers
    ]
    for copy in ag_copies:
        copy.start()

    for copy in gt_copies:
        copy.wait()
    gate_radius = gate[0]
    for slot in range(1, count_gen):
        gate_radius = gate_radius + gate[slot]
    gate_center, slope_val, spread_term = relax_gate(ex_center, gate_radius)
    gates_ref[...] = (slope_val * ex_gens)[:, None, :]
    gate_total = slope_val * gate_radius + spread_term
    stats_ref[0:1] = gate_center
    stats_ref[1:2] = spread_term
    stats_ref[2:3] = gate_total
    for copy in ag_copies:
        copy.wait()
    feat_ref[...] = full_rad[:tiles].astype(jnp.float32).reshape(rows, cols, chans)


def exchange_call(mesh, radius, sum_gens, sum_center, w_reduce, w_excite, vectors):
    rows, cols, chans = radius.shape
    gens = sum_gens.shape[0]
    count_gen, count_row, count_ch = mesh["gen"], mesh["row"], mesh["ch"]
    per = -(-(rows * cols // 8) // count_gen)
    units = w_reduce.shape[1]
    vmem = pl.BlockSpec(memory_space=pltpu.VMEM)
    side = count_row * count_ch
    dma = pltpu.SemaphoreType.DMA
    return pl.pallas_call(
        functools.partial(exchange_kernel, gens, rows, cols, count_gen, count_row, count_ch, per),
        in_specs=[vmem] * 6,
        out_specs=[vmem] * 3,
        out_shape=[
            jax.ShapeDtypeStruct((gens, 1, chans), jnp.float32),
            jax.ShapeDtypeStruct((3, chans), jnp.float32),
            jax.ShapeDtypeStruct((rows, cols, chans), jnp.float32),
        ],
        scratch_shapes=[
            pltpu.VMEM((count_gen * per, 8, chans), jnp.bfloat16),
            pltpu.VMEM((count_gen, per, 8, chans), jnp.bfloat16),
            pltpu.VMEM((count_gen * per, 8, chans), jnp.bfloat16),
            pltpu.VMEM((side, gens + 8, units), jnp.float32),
            pltpu.VMEM((count_gen, 1, chans), jnp.float32),
            dma((count_gen,)), dma((count_gen,)), dma((count_gen,)), dma((count_gen,)),
            dma((side,)), dma((side,)), dma((count_gen,)), dma((count_gen,)),
        ],
        compiler_params=pltpu.CompilerParams(
            collective_id=1, has_side_effects=True, vmem_limit_bytes=32 << 20
        ),
    )(radius, sum_gens, sum_center, w_reduce, w_excite, vectors)


def final_kernel(block, dwg_ref, gates_ref, dwc_ref, feat_ref, stats_ref, oc_ref, og_ref, ob_ref):
    center = dwc_ref[...]
    gate_center = stats_ref[0:1]

    @pl.when(pl.program_id(0) == 0)
    def _():
        oc_ref[...] = center * gate_center
        ob_ref[...] = jnp.abs(center) * stats_ref[1:2] + feat_ref[...] * stats_ref[2:3]

    for k in range(block):
        og_ref[k] = (
            center * gates_ref[k] + gate_center * dwg_ref[k].astype(jnp.float32)
        ).astype(jnp.bfloat16)


def final_call(dw_gens, gates, dw_center, feat, stats):
    gens, rows, cols, chans = dw_gens.shape
    block = 8
    whole = pl.BlockSpec((rows, cols, chans), lambda i: (0, 0, 0))
    big = pl.BlockSpec((block, rows, cols, chans), lambda i: (i, 0, 0, 0))
    return pl.pallas_call(
        functools.partial(final_kernel, block),
        grid=(gens // block,),
        in_specs=[
            big,
            pl.BlockSpec((block, 1, chans), lambda i: (i, 0, 0)),
            whole,
            whole,
            pl.BlockSpec((3, chans), lambda i: (0, 0)),
        ],
        out_specs=[whole, big, whole],
        out_shape=[
            jax.ShapeDtypeStruct((rows, cols, chans), jnp.float32),
            jax.ShapeDtypeStruct(dw_gens.shape, jnp.bfloat16),
            jax.ShapeDtypeStruct((rows, cols, chans), jnp.float32),
        ],
        compiler_params=pltpu.CompilerParams(
            dimension_semantics=("arbitrary",), vmem_limit_bytes=32 << 20
        ),
    )(dw_gens, gates, dw_center, feat, stats)


def merged_weights(w_expand, b_expand, w_depth):
    taps = w_depth.shape[0]
    c_in, chans = w_expand.shape
    wide = -(-chans // LANES) * LANES
    bias = b_expand.astype(jnp.bfloat16)
    rest = (b_expand - bias.astype(jnp.float32)).astype(jnp.bfloat16)
    mixed = jnp.concatenate([w_expand, bias[None], rest[None]], axis=0)
    mixed = jnp.pad(mixed, ((0, LANES - c_in - 2), (0, wide - chans))).astype(jnp.float32)
    depth = jnp.pad(w_depth, ((0, 0), (0, 0), (0, wide - chans))).transpose(1, 0, 2)
    merged = (depth[:, :, None, :] * mixed[None, None]).astype(jnp.bfloat16)
    return merged.reshape(taps, taps * LANES, wide)


def halo_kernel(count_row, count_ch, margin, x_ref, out_ref, zero_ref, local_sem, send_sem, recv_sem, fwd_send, fwd_recv):
    rows = x_ref.shape[0]
    per = margin // count_ch
    my_row = lax.axis_index("row")
    my_ch = lax.axis_index("ch")
    has_up = my_row > 0
    has_down = my_row < count_row - 1
    barrier = pltpu.get_barrier_semaphore()
    places = [{"row": lax.rem(my_row + off, count_row)} for off in sorted({1, count_row - 1})]
    places += [{"ch": lax.rem(my_ch + off, count_ch)} for off in range(1, count_ch)]
    for place in places:
        pl.semaphore_signal(barrier, inc=1, device_id=place, device_id_type=MESH)

    inner = pltpu.make_async_copy(x_ref, out_ref.at[pl.ds(margin, rows)], local_sem.at[0])
    inner.start()
    zero_ref[...] = jnp.zeros_like(zero_ref)
    pl.semaphore_wait(barrier, len(places))

    part = my_ch * per
    above = pl.ds(part, per)
    below = pl.ds(margin + rows + part, per)

    def sent_down():
        return pltpu.make_async_remote_copy(
            src_ref=x_ref.at[pl.ds(rows - margin + part, per)], dst_ref=out_ref.at[above],
            send_sem=send_sem.at[0], recv_sem=recv_sem.at[0],
            device_id={"row": lax.rem(my_row + 1, count_row)}, device_id_type=MESH,
        )

    def sent_up():
        return pltpu.make_async_remote_copy(
            src_ref=x_ref.at[pl.ds(part, per)], dst_ref=out_ref.at[below],
            send_sem=send_sem.at[1], recv_sem=recv_sem.at[1],
            device_id={"row": lax.rem(my_row + count_row - 1, count_row)}, device_id_type=MESH,
        )

    def forwards(side):
        where = (above, below)[side]
        return [
            pltpu.make_async_remote_copy(
                src_ref=out_ref.at[where], dst_ref=out_ref.at[where],
                send_sem=fwd_send.at[side, off], recv_sem=fwd_recv.at[side, off],
                device_id={"ch": lax.rem(my_ch + off, count_ch)}, device_id_type=MESH,
            )
            for off in range(1, count_ch)
        ]

    def fill(side):
        start = (0, margin + rows)[side]
        return pltpu.make_async_copy(
            zero_ref, out_ref.at[pl.ds(start, margin)], local_sem.at[1 + side]
        )

    for present, send in ((has_down, sent_down), (has_up, sent_up)):
        @pl.when(present)
        def _(send=send):
            send().start()

    for side, present, send in ((0, has_up, sent_down), (1, has_down, sent_up)):
        @pl.when(present)
        def _(side=side, send=send):
            send().wait_recv()
            for copy in forwards(side):
                copy.start()

        @pl.when(jnp.logical_not(present))
        def _(side=side):
            fill(side).start()

    for side, present in ((0, has_up), (1, has_down)):
        @pl.when(present)
        def _(side=side):
            for copy in forwards(side):
                copy.wait()

        @pl.when(jnp.logical_not(present))
        def _(side=side):
            fill(side).wait()

    for present, send in ((has_down, sent_down), (has_up, sent_up)):
        @pl.when(present)
        def _(send=send):
            send().wait_send()
    inner.wait()


def halo_call(mesh, flat, margin):
    rows, span, lanes = flat.shape
    anywhere = pl.BlockSpec(memory_space=pl.ANY)
    dma = pltpu.SemaphoreType.DMA
    return pl.pallas_call(
        functools.partial(halo_kernel, mesh["row"], mesh["ch"], margin),
        in_specs=[anywhere],
        out_specs=anywhere,
        out_shape=jax.ShapeDtypeStruct((rows + 2 * margin, span, lanes), flat.dtype),
        scratch_shapes=[
            pltpu.VMEM((margin, span, lanes), flat.dtype),
            dma((3,)), dma((2,)), dma((2,)), dma((2, mesh["ch"])), dma((2, mesh["ch"])),
        ],
        compiler_params=pltpu.CompilerParams(collective_id=2, has_side_effects=True),
    )(flat)


def on_device(
    shape, x_center, x_gens, w_expand, b_expand, w_depth, b_depth, w_reduce, b_reduce, w_excite, b_excite
):
    gens, rows, cols, c_in = x_gens.shape
    chans = w_expand.shape[1]
    taps = w_depth.shape[0]
    margin = taps // 2
    weights = merged_weights(w_expand, b_expand, w_depth)
    ones = jnp.ones((rows, cols, 2), jnp.bfloat16)
    center = jnp.concatenate([x_center, ones], axis=-1)
    center = jnp.pad(center, ((0, 0), (0, cols), (0, LANES - c_in - 2)))
    flat = x_gens.transpose(1, 0, 2, 3).reshape(rows, gens * cols, c_in)
    flat = jnp.concatenate([jnp.pad(flat, ((0, 0), (0, 0), (0, LANES - c_in))), center], axis=1)
    x_rows = halo_call(shape, flat, margin)
    units = b_reduce.shape[0]
    vectors = jnp.stack([b_depth, b_excite, jnp.pad(b_reduce, (0, chans - units))])
    dw_gens, dw_center, local_radius, sum_gens, sum_center = conv_call(
        x_rows, weights, vectors, gens, rows, taps, cols
    )
    gates, stats, feat = exchange_call(
        shape, local_radius, sum_gens, sum_center, w_reduce, w_excite, vectors
    )
    return final_call(dw_gens, gates, dw_center, feat, stats)


def solution(mesh):
    in_specs = (
        P(("grp", "row"), None, None),
        P(("grp", "gen"), "row", None, None),
        P(None, "ch"),
        P("ch"),
        P(None, None, "ch"),
        P("ch"),
        P(),
        P(),
        P(None, "ch"),
        P("ch"),
    )
    out_specs = (
        P(("grp", "row"), None, "ch"),
        P(("grp", "gen"), "row", None, "ch"),
        P(("grp", "row"), None, "ch"),
    )
    return jax.shard_map(
        functools.partial(on_device, dict(mesh.shape)), mesh=mesh, in_specs=in_specs, out_specs=out_specs, check_vma=False
    )
```

```python
import functools

import jax
import jax.numpy as jnp
from jax import lax
from jax.experimental import pallas as pl
from jax.experimental.pallas import tpu as pltpu
from jax.sharding import PartitionSpec as P

MESH = pl.DeviceIdType.MESH
LANES = 128
BLOCK = 4


def conv_rows(source, w_ref, shifted_ref, acc_ref, rows, taps, cols):
    margin = taps // 2
    depth, span, lanes = source.shape
    values = source.astype(jnp.float32).reshape(depth * span, lanes)
    col = lax.broadcasted_iota(jnp.int32, (depth * span, lanes), 0) % cols
    for tap_col in range(taps):
        shift = tap_col - margin
        moved = values
        if shift != 0:
            moved = pltpu.roll(values, (-shift) % (depth * span), 0)
            keep = (col + shift >= 0) & (col + shift < cols)
            moved = jnp.where(keep, moved, 0.0)
        shifted_ref[:, :span, :] = moved.astype(jnp.bfloat16).reshape(depth, span, lanes)
        lhs = jnp.concatenate(
            [
                shifted_ref[tap_row : tap_row + rows, :span, :].reshape(rows * span, lanes)
                for tap_row in range(taps)
            ],
            axis=-1,
        )
        part = jnp.dot(lhs, w_ref[tap_col], preferred_element_type=jnp.float32)
        if tap_col == 0:
            acc_ref[: rows * span, :] = part
        else:
            acc_ref[: rows * span, :] += part


def conv_kernel(
    rows, taps, cols, block, chans,
    x_ref, w_ref, bd_ref,
    dwg_ref, dwc_ref, rad_ref, pg_ref, pc_ref,
    shifted_ref, acc_ref,
):
    step = pl.program_id(0)

    @pl.when(step == 0)
    def _():
        conv_rows(x_ref[:, -2 * cols :], w_ref, shifted_ref, acc_ref, rows, taps, cols)
        total = jnp.zeros((cols, chans), jnp.float32)
        for row in range(rows):
            one = acc_ref[row * 2 * cols : row * 2 * cols + cols, :chans] + bd_ref[0:1]
            dwc_ref[row] = one
            total = total + one
        pc_ref[...] = jnp.sum(total, axis=0, keepdims=True)
        rad_ref[...] = jnp.zeros_like(rad_ref)

    span = block * cols
    here = pl.ds(pl.multiple_of(step * span, span), span)
    conv_rows(x_ref[:, here], w_ref, shifted_ref, acc_ref, rows, taps, cols)
    totals = [jnp.zeros((cols, chans), jnp.float32) for _ in range(block)]
    for row in range(rows):
        radius = rad_ref[row]
        for k in range(block):
            start = (row * block + k) * cols
            one = acc_ref[start : start + cols, :chans].astype(jnp.bfloat16)
            dwg_ref[k, row] = one
            wide = one.astype(jnp.float32)
            radius = radius + jnp.abs(wide)
            totals[k] = totals[k] + wide
        rad_ref[row] = radius
    for k in range(block):
        pg_ref[k] = jnp.sum(totals[k], axis=0, keepdims=True)


def conv_call(x_rows, weights, vectors, gens, rows, taps, cols):
    chans = vectors.shape[1]
    depth = rows + taps - 1
    wide = weights.shape[-1]
    block = BLOCK
    return pl.pallas_call(
        functools.partial(conv_kernel, rows, taps, cols, block, chans),
        grid=(gens // block,),
        in_specs=[
            pl.BlockSpec(memory_space=pltpu.VMEM),
            pl.BlockSpec(memory_space=pltpu.VMEM),
            pl.BlockSpec(vectors.shape, lambda i: (0, 0)),
        ],
        out_specs=[
            pl.BlockSpec((block, rows, cols, chans), lambda i: (i, 0, 0, 0)),
            pl.BlockSpec((rows, cols, chans), lambda i: (0, 0, 0)),
            pl.BlockSpec((rows, cols, chans), lambda i: (0, 0, 0)),
            pl.BlockSpec((block, 1, chans), lambda i: (i, 0, 0)),
            pl.BlockSpec((1, chans), lambda i: (0, 0)),
        ],
        out_shape=[
            jax.ShapeDtypeStruct((gens, rows, cols, chans), jnp.bfloat16),
            jax.ShapeDtypeStruct((rows, cols, chans), jnp.float32),
            jax.ShapeDtypeStruct((rows, cols, chans), jnp.float32),
            jax.ShapeDtypeStruct((gens, 1, chans), jnp.float32),
            jax.ShapeDtypeStruct((1, chans), jnp.float32),
        ],
        scratch_shapes=[
            pltpu.VMEM((depth, block * cols, LANES), jnp.bfloat16),
            pltpu.VMEM((rows * block * cols, wide), jnp.float32),
        ],
        compiler_params=pltpu.CompilerParams(
            dimension_semantics=("arbitrary",), vmem_limit_bytes=20 << 20
        ),
        cost_estimate=pl.CostEstimate(
            flops=2 * gens * rows * cols * taps * taps * LANES * wide,
            bytes_accessed=10 << 20,
            transcendentals=0,
        ),
    )(x_rows, weights, vectors)


def relax_gate(ex_center, gate_radius):
    low_end = ex_center - gate_radius
    high_end = ex_center + gate_radius
    sig_low = jax.nn.sigmoid(low_end)
    sig_high = jax.nn.sigmoid(high_end)
    slope_val = jnp.minimum(sig_low * (1.0 - sig_low), sig_high * (1.0 - sig_high))
    gate_center = slope_val * ex_center + 0.5 * (
        sig_high + sig_low - slope_val * (high_end + low_end)
    )
    spread_term = 0.5 * (sig_high - sig_low - slope_val * (high_end - low_end))
    return (gate_center, slope_val, spread_term)


def exchange_kernel(
    gens, rows, cols, count_gen, count_row, count_ch, per,
    rad_ref, sg_ref, sc_ref, wr_ref, we_ref, vec_ref,
    gates_ref, stats_ref, feat_ref,
    send_rad, recv_rad, full_rad, squeeze, gate,
    rs_send, rs_recv, ag_send, ag_recv, sq_send, sq_recv, gt_send, gt_recv,
):
    my_gen = lax.axis_index("gen")
    my_row = lax.axis_index("row")
    my_ch = lax.axis_index("ch")
    chans = stats_ref.shape[-1]
    units = we_ref.shape[0]
    cells = rows * cols * count_row
    gen_peers = [(off, {"gen": lax.rem(my_gen + off, count_gen)}) for off in range(1, count_gen)]
    side_peers = []
    for off_row in range(count_row):
        for off_ch in range(count_ch):
            if off_row or off_ch:
                place = {
                    "row": lax.rem(my_row + off_row, count_row),
                    "ch": lax.rem(my_ch + off_ch, count_ch),
                }
                side_peers.append((off_row * count_ch + off_ch, place))
    barrier = pltpu.get_barrier_semaphore()
    for _, place in gen_peers + side_peers:
        pl.semaphore_signal(barrier, inc=1, device_id=place, device_id_type=MESH)

    pooled = jnp.concatenate(
        [sg_ref[...][:, 0], sc_ref[...], jnp.zeros((7, chans), jnp.float32)], axis=0
    ) * (1.0 / cells)
    own = wr_ref[:, :chans]
    for other in range(1, count_ch):
        own = jnp.where(my_ch == other, wr_ref[:, other * chans : (other + 1) * chans], own)
    part = lax.dot_general(
        pooled,
        own,
        (((1,), (1,)), ((), ())),
        precision=lax.Precision.HIGHEST,
        preferred_element_type=jnp.float32,
    )
    mine = my_row * count_ch + my_ch
    squeeze[mine] = part
    tiles = rows * cols // 8
    send_rad[:tiles] = rad_ref[...].reshape(tiles, 8, chans).astype(jnp.bfloat16)
    if count_gen * per > tiles:
        send_rad[tiles:] = jnp.zeros((count_gen * per - tiles, 8, chans), jnp.bfloat16)
    recv_rad[my_gen] = send_rad[pl.ds(my_gen * per, per)]

    pl.semaphore_wait(barrier, len(gen_peers) + len(side_peers))

    def remote(src, dst, send_sem, recv_sem, place):
        return pltpu.make_async_remote_copy(
            src_ref=src, dst_ref=dst, send_sem=send_sem, recv_sem=recv_sem,
            device_id=place, device_id_type=MESH,
        )

    sq_copies = [
        remote(squeeze.at[mine], squeeze.at[mine], sq_send.at[off], sq_recv.at[off], place)
        for off, place in side_peers
    ]
    rs_copies = [
        remote(
            send_rad.at[pl.ds(place["gen"] * per, per)], recv_rad.at[my_gen],
            rs_send.at[off], rs_recv.at[off], place,
        )
        for off, place in gen_peers
    ]
    for copy in sq_copies + rs_copies:
        copy.start()
    for copy in sq_copies:
        copy.wait()
    total = squeeze[0]
    for slot in range(1, count_row * count_ch):
        total = total + squeeze[slot]
    row_of = lax.broadcasted_iota(jnp.int32, total.shape, 0)
    total = total + jnp.where(row_of == gens, vec_ref[2:3, :units], 0.0)
    ex_all = jnp.dot(
        total, we_ref[...], precision=lax.Precision.HIGHEST, preferred_element_type=jnp.float32
    )
    ex_gens = ex_all[:gens]
    ex_center = ex_all[gens : gens + 1] + vec_ref[1:2]
    gate[my_gen] = jnp.sum(jnp.abs(ex_gens), axis=0, keepdims=True)
    gt_copies = [
        remote(gate.at[my_gen], gate.at[my_gen], gt_send.at[off], gt_recv.at[off], place)
        for off, place in gen_peers
    ]
    for copy in gt_copies:
        copy.start()

    for copy in rs_copies:
        copy.wait()
    chunk = recv_rad[0].astype(jnp.float32)
    for slot in range(1, count_gen):
        chunk = chunk + recv_rad[slot].astype(jnp.float32)
    own = pl.ds(my_gen * per, per)
    full_rad[own] = chunk.astype(jnp.bfloat16)
    ag_copies = [
        remote(full_rad.at[own], full_rad.at[own], ag_send.at[off], ag_recv.at[off], place)
        for off, place in gen_peers
    ]
    for copy in ag_copies:
        copy.start()

    for copy in gt_copies:
        copy.wait()
    gate_radius = gate[0]
    for slot in range(1, count_gen):
        gate_radius = gate_radius + gate[slot]
    gate_center, slope_val, spread_term = relax_gate(ex_center, gate_radius)
    gates_ref[...] = (slope_val * ex_gens)[:, None, :]
    gate_total = slope_val * gate_radius + spread_term
    stats_ref[0:1] = gate_center
    stats_ref[1:2] = spread_term
    stats_ref[2:3] = gate_total
    for copy in ag_copies:
        copy.wait()
    feat_ref[...] = full_rad[:tiles].astype(jnp.float32).reshape(rows, cols, chans)


def exchange_call(mesh, radius, sum_gens, sum_center, w_reduce, w_excite, vectors):
    rows, cols, chans = radius.shape
    gens = sum_gens.shape[0]
    count_gen, count_row, count_ch = mesh["gen"], mesh["row"], mesh["ch"]
    per = -(-(rows * cols // 8) // count_gen)
    units = w_excite.shape[0]
    vmem = pl.BlockSpec(memory_space=pltpu.VMEM)
    side = count_row * count_ch
    dma = pltpu.SemaphoreType.DMA
    return pl.pallas_call(
        functools.partial(exchange_kernel, gens, rows, cols, count_gen, count_row, count_ch, per),
        in_specs=[vmem] * 6,
        out_specs=[vmem] * 3,
        out_shape=[
            jax.ShapeDtypeStruct((gens, 1, chans), jnp.float32),
            jax.ShapeDtypeStruct((3, chans), jnp.float32),
            jax.ShapeDtypeStruct((rows, cols, chans), jnp.float32),
        ],
        scratch_shapes=[
            pltpu.VMEM((count_gen * per, 8, chans), jnp.bfloat16),
            pltpu.VMEM((count_gen, per, 8, chans), jnp.bfloat16),
            pltpu.VMEM((count_gen * per, 8, chans), jnp.bfloat16),
            pltpu.VMEM((side, gens + 8, units), jnp.float32),
            pltpu.VMEM((count_gen, 1, chans), jnp.float32),
            dma((count_gen,)), dma((count_gen,)), dma((count_gen,)), dma((count_gen,)),
            dma((side,)), dma((side,)), dma((count_gen,)), dma((count_gen,)),
        ],
        compiler_params=pltpu.CompilerParams(
            collective_id=1, has_side_effects=True, vmem_limit_bytes=12 << 20
        ),
    )(radius, sum_gens, sum_center, w_reduce, w_excite, vectors)


def final_kernel(block, dwg_ref, gates_ref, dwc_ref, feat_ref, stats_ref, oc_ref, og_ref, ob_ref):
    center = dwc_ref[...]
    gate_center = stats_ref[0:1]

    @pl.when(pl.program_id(0) == 0)
    def _():
        oc_ref[...] = center * gate_center
        ob_ref[...] = jnp.abs(center) * stats_ref[1:2] + feat_ref[...] * stats_ref[2:3]

    for k in range(block):
        og_ref[k] = (
            center * gates_ref[k] + gate_center * dwg_ref[k].astype(jnp.float32)
        ).astype(jnp.bfloat16)


def final_call(dw_gens, gates, dw_center, feat, stats):
    gens, rows, cols, chans = dw_gens.shape
    block = 8
    whole = pl.BlockSpec((rows, cols, chans), lambda i: (0, 0, 0))
    big = pl.BlockSpec((block, rows, cols, chans), lambda i: (i, 0, 0, 0))
    return pl.pallas_call(
        functools.partial(final_kernel, block),
        grid=(gens // block,),
        in_specs=[
            big,
            pl.BlockSpec((block, 1, chans), lambda i: (i, 0, 0)),
            whole,
            whole,
            pl.BlockSpec((3, chans), lambda i: (0, 0)),
        ],
        out_specs=[whole, big, whole],
        out_shape=[
            jax.ShapeDtypeStruct((rows, cols, chans), jnp.float32),
            jax.ShapeDtypeStruct(dw_gens.shape, jnp.bfloat16),
            jax.ShapeDtypeStruct((rows, cols, chans), jnp.float32),
        ],
        compiler_params=pltpu.CompilerParams(
            dimension_semantics=("arbitrary",), vmem_limit_bytes=12 << 20
        ),
    )(dw_gens, gates, dw_center, feat, stats)


def merged_weights(w_expand, b_expand, w_depth):
    taps = w_depth.shape[0]
    c_in, chans = w_expand.shape
    wide = -(-chans // LANES) * LANES
    bias = b_expand.astype(jnp.bfloat16)
    rest = (b_expand - bias.astype(jnp.float32)).astype(jnp.bfloat16)
    mixed = jnp.concatenate([w_expand, bias[None], rest[None]], axis=0)
    mixed = jnp.pad(mixed, ((0, LANES - c_in - 2), (0, wide - chans))).astype(jnp.float32)
    depth = jnp.pad(w_depth, ((0, 0), (0, 0), (0, wide - chans))).transpose(1, 0, 2)
    merged = (depth[:, :, None, :] * mixed[None, None]).astype(jnp.bfloat16)
    return merged.reshape(taps, taps * LANES, wide)


def halo_kernel(count_row, count_ch, margin, x_ref, out_ref, send_sem, recv_sem, fwd_send, fwd_recv):
    rows = x_ref.shape[0]
    per = margin // count_ch
    my_row = lax.axis_index("row")
    my_ch = lax.axis_index("ch")
    has_up = my_row > 0
    has_down = my_row < count_row - 1
    barrier = pltpu.get_barrier_semaphore()
    places = [{"row": lax.rem(my_row + off, count_row)} for off in sorted({1, count_row - 1})]
    places += [{"ch": lax.rem(my_ch + off, count_ch)} for off in range(1, count_ch)]
    for place in places:
        pl.semaphore_signal(barrier, inc=1, device_id=place, device_id_type=MESH)

    pl.semaphore_wait(barrier, len(places))

    part = my_ch * per
    above = pl.ds(part, per)
    below = pl.ds(margin + rows + part, per)

    def sent_down():
        return pltpu.make_async_remote_copy(
            src_ref=x_ref.at[pl.ds(rows - margin + part, per)], dst_ref=out_ref.at[above],
            send_sem=send_sem.at[0], recv_sem=recv_sem.at[0],
            device_id={"row": lax.rem(my_row + 1, count_row)}, device_id_type=MESH,
        )

    def sent_up():
        return pltpu.make_async_remote_copy(
            src_ref=x_ref.at[pl.ds(part, per)], dst_ref=out_ref.at[below],
            send_sem=send_sem.at[1], recv_sem=recv_sem.at[1],
            device_id={"row": lax.rem(my_row + count_row - 1, count_row)}, device_id_type=MESH,
        )

    def forwards(side):
        where = (above, below)[side]
        return [
            pltpu.make_async_remote_copy(
                src_ref=out_ref.at[where], dst_ref=out_ref.at[where],
                send_sem=fwd_send.at[side, off], recv_sem=fwd_recv.at[side, off],
                device_id={"ch": lax.rem(my_ch + off, count_ch)}, device_id_type=MESH,
            )
            for off in range(1, count_ch)
        ]

    for present, send in ((has_down, sent_down), (has_up, sent_up)):
        @pl.when(present)
        def _(send=send):
            send().start()

    out_ref[margin : margin + rows] = x_ref[...]

    for side, present, send in ((0, has_up, sent_down), (1, has_down, sent_up)):
        @pl.when(present)
        def _(side=side, send=send):
            send().wait_recv()
            for copy in forwards(side):
                copy.start()

        @pl.when(jnp.logical_not(present))
        def _(side=side):
            start = (0, margin + rows)[side]
            out_ref[start : start + margin] = jnp.zeros((margin,) + x_ref.shape[1:], x_ref.dtype)

    for side, present in ((0, has_up), (1, has_down)):
        @pl.when(present)
        def _(side=side):
            for copy in forwards(side):
                copy.wait()

    for present, send in ((has_down, sent_down), (has_up, sent_up)):
        @pl.when(present)
        def _(send=send):
            send().wait_send()


def halo_call(mesh, flat, margin):
    rows, span, lanes = flat.shape
    anywhere = pl.BlockSpec(memory_space=pltpu.VMEM)
    dma = pltpu.SemaphoreType.DMA
    return pl.pallas_call(
        functools.partial(halo_kernel, mesh["row"], mesh["ch"], margin),
        in_specs=[anywhere],
        out_specs=anywhere,
        out_shape=jax.ShapeDtypeStruct((rows + 2 * margin, span, lanes), flat.dtype),
        scratch_shapes=[
            dma((2,)), dma((2,)), dma((2, mesh["ch"])), dma((2, mesh["ch"])),
        ],
        compiler_params=pltpu.CompilerParams(
            collective_id=2, has_side_effects=True, vmem_limit_bytes=12 << 20
        ),
    )(flat)


def on_device(
    shape, x_center, x_gens, w_expand, b_expand, w_depth, b_depth, w_reduce, b_reduce, w_excite, b_excite
):
    gens, rows, cols, c_in = x_gens.shape
    chans = w_expand.shape[1]
    taps = w_depth.shape[0]
    margin = taps // 2
    weights = merged_weights(w_expand, b_expand, w_depth)
    ones = jnp.ones((rows, cols, 2), jnp.bfloat16)
    center = jnp.concatenate([x_center, ones], axis=-1)
    center = jnp.pad(center, ((0, 0), (0, cols), (0, LANES - c_in - 2)))
    flat = x_gens.transpose(1, 0, 2, 3).reshape(rows, gens * cols, c_in)
    flat = jnp.concatenate([jnp.pad(flat, ((0, 0), (0, 0), (0, LANES - c_in))), center], axis=1)
    x_rows = halo_call(shape, flat, margin)
    units = b_reduce.shape[0]
    vectors = jnp.stack([b_depth, b_excite, jnp.pad(b_reduce, (0, chans - units))])
    dw_gens, dw_center, local_radius, sum_gens, sum_center = conv_call(
        x_rows, weights, vectors, gens, rows, taps, cols
    )
    gates, stats, feat = exchange_call(
        shape, local_radius, sum_gens, sum_center, w_reduce.T, w_excite, vectors
    )
    return final_call(dw_gens, gates, dw_center, feat, stats)


def solution(mesh):
    in_specs = (
        P(("grp", "row"), None, None),
        P(("grp", "gen"), "row", None, None),
        P(None, "ch"),
        P("ch"),
        P(None, None, "ch"),
        P("ch"),
        P(),
        P(),
        P(None, "ch"),
        P("ch"),
    )
    out_specs = (
        P(("grp", "row"), None, "ch"),
        P(("grp", "gen"), "row", None, "ch"),
        P(("grp", "row"), None, "ch"),
    )
    return jax.shard_map(
        functools.partial(on_device, dict(mesh.shape)), mesh=mesh, in_specs=in_specs, out_specs=out_specs, check_vma=False
    )
```

```python
import functools

import jax
import jax.numpy as jnp
from jax import lax
from jax.experimental import pallas as pl
from jax.experimental.pallas import tpu as pltpu
from jax.sharding import PartitionSpec as P

MESH = pl.DeviceIdType.MESH
LANES = 128
BLOCK = 8


def conv_rows(source, w_ref, shifted_ref, acc_ref, rows, taps, cols):
    margin = taps // 2
    depth, span, lanes = source.shape
    values = source.astype(jnp.float32).reshape(depth * span, lanes)
    col = lax.broadcasted_iota(jnp.int32, (depth * span, lanes), 0) % cols
    for tap_col in range(taps):
        shift = tap_col - margin
        moved = values
        if shift != 0:
            moved = pltpu.roll(values, (-shift) % (depth * span), 0)
            keep = (col + shift >= 0) & (col + shift < cols)
            moved = jnp.where(keep, moved, 0.0)
        shifted_ref[tap_col, :, :span, :] = moved.astype(jnp.bfloat16).reshape(depth, span, lanes)
    lhs = jnp.concatenate(
        [
            shifted_ref[tap_col, tap_row : tap_row + rows, :span, :].reshape(rows * span, lanes)
            for tap_col in range(taps)
            for tap_row in range(taps)
        ],
        axis=-1,
    )
    acc_ref[: rows * span, :] = jnp.dot(lhs, w_ref[...], preferred_element_type=jnp.float32)


def conv_kernel(
    rows, taps, cols, block, chans,
    x_ref, w_ref, bd_ref,
    dwg_ref, dwc_ref, rad_ref, pg_ref, pc_ref,
    shifted_ref, acc_ref,
):
    step = pl.program_id(0)

    @pl.when(step == 0)
    def _():
        conv_rows(x_ref[:, -2 * cols :], w_ref, shifted_ref, acc_ref, rows, taps, cols)
        total = jnp.zeros((cols, chans), jnp.float32)
        for row in range(rows):
            one = acc_ref[row * 2 * cols : row * 2 * cols + cols, :chans] + bd_ref[...][None, :]
            dwc_ref[row] = one
            total = total + one
        pc_ref[...] = jnp.sum(total, axis=0, keepdims=True)
        rad_ref[...] = jnp.zeros_like(rad_ref)

    span = block * cols
    here = pl.ds(pl.multiple_of(step * span, span), span)
    conv_rows(x_ref[:, here], w_ref, shifted_ref, acc_ref, rows, taps, cols)
    totals = [jnp.zeros((cols, chans), jnp.float32) for _ in range(block)]
    for row in range(rows):
        radius = rad_ref[row]
        for k in range(block):
            start = (row * block + k) * cols
            one = acc_ref[start : start + cols, :chans].astype(jnp.bfloat16)
            dwg_ref[k, row] = one
            wide = one.astype(jnp.float32)
            radius = radius + jnp.abs(wide)
            totals[k] = totals[k] + wide
        rad_ref[row] = radius
    for k in range(block):
        pg_ref[k] = jnp.sum(totals[k], axis=0, keepdims=True)


def conv_call(x_rows, weights, b_depth, gens, rows, taps, cols):
    chans = b_depth.shape[0]
    depth = rows + taps - 1
    wide = weights.shape[-1]
    block = BLOCK
    return pl.pallas_call(
        functools.partial(conv_kernel, rows, taps, cols, block, chans),
        grid=(gens // block,),
        in_specs=[
            pl.BlockSpec(memory_space=pltpu.VMEM),
            pl.BlockSpec(memory_space=pltpu.VMEM),
            pl.BlockSpec(memory_space=pltpu.VMEM),
        ],
        out_specs=[
            pl.BlockSpec((block, rows, cols, chans), lambda i: (i, 0, 0, 0)),
            pl.BlockSpec((rows, cols, chans), lambda i: (0, 0, 0)),
            pl.BlockSpec((rows, cols, chans), lambda i: (0, 0, 0)),
            pl.BlockSpec((block, 1, chans), lambda i: (i, 0, 0)),
            pl.BlockSpec((1, chans), lambda i: (0, 0)),
        ],
        out_shape=[
            jax.ShapeDtypeStruct((gens, rows, cols, chans), jnp.bfloat16),
            jax.ShapeDtypeStruct((rows, cols, chans), jnp.float32),
            jax.ShapeDtypeStruct((rows, cols, chans), jnp.float32),
            jax.ShapeDtypeStruct((gens, 1, chans), jnp.float32),
            jax.ShapeDtypeStruct((1, chans), jnp.float32),
        ],
        scratch_shapes=[
            pltpu.VMEM((taps, depth, block * cols, LANES), jnp.bfloat16),
            pltpu.VMEM((rows * block * cols, wide), jnp.float32),
        ],
        compiler_params=pltpu.CompilerParams(
            dimension_semantics=("arbitrary",), vmem_limit_bytes=32 << 20
        ),
        cost_estimate=pl.CostEstimate(
            flops=2 * gens * rows * cols * taps * taps * LANES * wide,
            bytes_accessed=10 << 20,
            transcendentals=0,
        ),
    )(x_rows, weights, b_depth)


def relax_gate(ex_center, gate_radius):
    low_end = ex_center - gate_radius
    high_end = ex_center + gate_radius
    sig_low = jax.nn.sigmoid(low_end)
    sig_high = jax.nn.sigmoid(high_end)
    slope_val = jnp.minimum(sig_low * (1.0 - sig_low), sig_high * (1.0 - sig_high))
    gate_center = slope_val * ex_center + 0.5 * (
        sig_high + sig_low - slope_val * (high_end + low_end)
    )
    spread_term = 0.5 * (sig_high - sig_low - slope_val * (high_end - low_end))
    return (gate_center, slope_val, spread_term)


def exchange_kernel(
    gens, rows, cols, count_gen, count_row, count_ch, per,
    rad_ref, sg_ref, sc_ref, wr_ref, br_ref, we_ref, be_ref,
    gates_ref, stats_ref, feat_ref,
    send_rad, recv_rad, full_rad, squeeze, gate,
    rs_send, rs_recv, ag_send, ag_recv, sq_send, sq_recv, gt_send, gt_recv,
):
    my_gen = lax.axis_index("gen")
    my_row = lax.axis_index("row")
    my_ch = lax.axis_index("ch")
    chans = stats_ref.shape[-1]
    cells = rows * cols * count_row
    gen_peers = [(off, {"gen": lax.rem(my_gen + off, count_gen)}) for off in range(1, count_gen)]
    side_peers = []
    for off_row in range(count_row):
        for off_ch in range(count_ch):
            if off_row or off_ch:
                place = {
                    "row": lax.rem(my_row + off_row, count_row),
                    "ch": lax.rem(my_ch + off_ch, count_ch),
                }
                side_peers.append((off_row * count_ch + off_ch, place))
    barrier = pltpu.get_barrier_semaphore()
    for _, place in gen_peers + side_peers:
        pl.semaphore_signal(barrier, inc=1, device_id=place, device_id_type=MESH)

    pooled = jnp.concatenate(
        [sg_ref[...][:, 0], sc_ref[...], jnp.zeros((7, chans), jnp.float32)], axis=0
    ) * (1.0 / cells)
    own = wr_ref[:, :chans]
    for other in range(1, count_ch):
        own = jnp.where(my_ch == other, wr_ref[:, other * chans : (other + 1) * chans], own)
    part = lax.dot_general(
        pooled,
        own,
        (((1,), (1,)), ((), ())),
        precision=lax.Precision.HIGHEST,
        preferred_element_type=jnp.float32,
    )
    mine = my_row * count_ch + my_ch
    squeeze[mine] = part
    tiles = rows * cols // 8
    send_rad[:tiles] = rad_ref[...].reshape(tiles, 8, chans).astype(jnp.bfloat16)
    if count_gen * per > tiles:
        send_rad[tiles:] = jnp.zeros((count_gen * per - tiles, 8, chans), jnp.bfloat16)
    recv_rad[my_gen] = send_rad[pl.ds(my_gen * per, per)]

    pl.semaphore_wait(barrier, len(gen_peers) + len(side_peers))

    def remote(src, dst, send_sem, recv_sem, place):
        return pltpu.make_async_remote_copy(
            src_ref=src, dst_ref=dst, send_sem=send_sem, recv_sem=recv_sem,
            device_id=place, device_id_type=MESH,
        )

    sq_copies = [
        remote(squeeze.at[mine], squeeze.at[mine], sq_send.at[off], sq_recv.at[off], place)
        for off, place in side_peers
    ]
    rs_copies = [
        remote(
            send_rad.at[pl.ds(place["gen"] * per, per)], recv_rad.at[my_gen],
            rs_send.at[off], rs_recv.at[off], place,
        )
        for off, place in gen_peers
    ]
    for copy in sq_copies + rs_copies:
        copy.start()
    for copy in sq_copies:
        copy.wait()
    total = squeeze[0]
    for slot in range(1, count_row * count_ch):
        total = total + squeeze[slot]
    row_of = lax.broadcasted_iota(jnp.int32, total.shape, 0)
    total = total + jnp.where(row_of == gens, br_ref[...][None, :], 0.0)
    ex_all = jnp.dot(
        total, we_ref[...], precision=lax.Precision.HIGHEST, preferred_element_type=jnp.float32
    )
    ex_gens = ex_all[:gens]
    ex_center = ex_all[gens : gens + 1] + be_ref[...][None, :]
    gate[my_gen] = jnp.sum(jnp.abs(ex_gens), axis=0, keepdims=True)
    gt_copies = [
        remote(gate.at[my_gen], gate.at[my_gen], gt_send.at[off], gt_recv.at[off], place)
        for off, place in gen_peers
    ]
    for copy in gt_copies:
        copy.start()

    for copy in rs_copies:
        copy.wait()
    chunk = recv_rad[0].astype(jnp.float32)
    for slot in range(1, count_gen):
        chunk = chunk + recv_rad[slot].astype(jnp.float32)
    own = pl.ds(my_gen * per, per)
    full_rad[own] = chunk.astype(jnp.bfloat16)
    ag_copies = [
        remote(full_rad.at[own], full_rad.at[own], ag_send.at[off], ag_recv.at[off], place)
        for off, place in gen_peers
    ]
    for copy in ag_copies:
        copy.start()

    for copy in gt_copies:
        copy.wait()
    gate_radius = gate[0]
    for slot in range(1, count_gen):
        gate_radius = gate_radius + gate[slot]
    gate_center, slope_val, spread_term = relax_gate(ex_center, gate_radius)
    gates_ref[...] = (slope_val * ex_gens)[:, None, :]
    gate_total = slope_val * gate_radius + spread_term
    stats_ref[0:1] = gate_center
    stats_ref[1:2] = spread_term
    stats_ref[2:3] = gate_total
    for copy in ag_copies:
        copy.wait()
    feat_ref[...] = full_rad[:tiles].astype(jnp.float32).reshape(rows, cols, chans)


def exchange_call(mesh, radius, sum_gens, sum_center, w_reduce, b_reduce, w_excite, b_excite):
    rows, cols, chans = radius.shape
    gens = sum_gens.shape[0]
    count_gen, count_row, count_ch = mesh["gen"], mesh["row"], mesh["ch"]
    per = -(-(rows * cols // 8) // count_gen)
    units = w_excite.shape[0]
    vmem = pl.BlockSpec(memory_space=pltpu.VMEM)
    side = count_row * count_ch
    dma = pltpu.SemaphoreType.DMA
    return pl.pallas_call(
        functools.partial(exchange_kernel, gens, rows, cols, count_gen, count_row, count_ch, per),
        in_specs=[vmem] * 7,
        out_specs=[vmem] * 3,
        out_shape=[
            jax.ShapeDtypeStruct((gens, 1, chans), jnp.float32),
            jax.ShapeDtypeStruct((3, chans), jnp.float32),
            jax.ShapeDtypeStruct((rows, cols, chans), jnp.float32),
        ],
        scratch_shapes=[
            pltpu.VMEM((count_gen * per, 8, chans), jnp.bfloat16),
            pltpu.VMEM((count_gen, per, 8, chans), jnp.bfloat16),
            pltpu.VMEM((count_gen * per, 8, chans), jnp.bfloat16),
            pltpu.VMEM((side, gens + 8, units), jnp.float32),
            pltpu.VMEM((count_gen, 1, chans), jnp.float32),
            dma((count_gen,)), dma((count_gen,)), dma((count_gen,)), dma((count_gen,)),
            dma((side,)), dma((side,)), dma((count_gen,)), dma((count_gen,)),
        ],
        compiler_params=pltpu.CompilerParams(
            collective_id=1, has_side_effects=True, vmem_limit_bytes=12 << 20
        ),
    )(radius, sum_gens, sum_center, w_reduce, b_reduce, w_excite, b_excite)


def final_kernel(block, dwg_ref, gates_ref, dwc_ref, feat_ref, stats_ref, oc_ref, og_ref, ob_ref):
    center = dwc_ref[...]
    gate_center = stats_ref[0:1]

    @pl.when(pl.program_id(0) == 0)
    def _():
        oc_ref[...] = center * gate_center
        ob_ref[...] = jnp.abs(center) * stats_ref[1:2] + feat_ref[...] * stats_ref[2:3]

    for k in range(block):
        og_ref[k] = (
            center * gates_ref[k] + gate_center * dwg_ref[k].astype(jnp.float32)
        ).astype(jnp.bfloat16)


def final_call(dw_gens, gates, dw_center, feat, stats):
    gens, rows, cols, chans = dw_gens.shape
    block = 8
    whole = pl.BlockSpec((rows, cols, chans), lambda i: (0, 0, 0))
    big = pl.BlockSpec((block, rows, cols, chans), lambda i: (i, 0, 0, 0))
    return pl.pallas_call(
        functools.partial(final_kernel, block),
        grid=(gens // block,),
        in_specs=[
            big,
            pl.BlockSpec((block, 1, chans), lambda i: (i, 0, 0)),
            whole,
            whole,
            pl.BlockSpec((3, chans), lambda i: (0, 0)),
        ],
        out_specs=[whole, big, whole],
        out_shape=[
            jax.ShapeDtypeStruct((rows, cols, chans), jnp.float32),
            jax.ShapeDtypeStruct(dw_gens.shape, jnp.bfloat16),
            jax.ShapeDtypeStruct((rows, cols, chans), jnp.float32),
        ],
        compiler_params=pltpu.CompilerParams(
            dimension_semantics=("arbitrary",), vmem_limit_bytes=12 << 20
        ),
    )(dw_gens, gates, dw_center, feat, stats)


def merged_weights(w_expand, b_expand, w_depth):
    taps = w_depth.shape[0]
    c_in, chans = w_expand.shape
    wide = -(-chans // LANES) * LANES
    mixed = jnp.concatenate([w_expand.astype(jnp.float32), b_expand[None]], axis=0)
    mixed = jnp.pad(mixed, ((0, LANES - c_in - 1), (0, wide - chans)))
    depth = jnp.pad(w_depth, ((0, 0), (0, 0), (0, wide - chans))).transpose(1, 0, 2)
    merged = (depth[:, :, None, :] * mixed[None, None]).astype(jnp.bfloat16)
    return merged.reshape(taps * taps * LANES, wide)


def halo_kernel(count_row, count_ch, margin, x_ref, out_ref, send_sem, recv_sem, fwd_send, fwd_recv):
    rows = x_ref.shape[0]
    per = margin // count_ch
    my_row = lax.axis_index("row")
    my_ch = lax.axis_index("ch")
    has_up = my_row > 0
    has_down = my_row < count_row - 1
    barrier = pltpu.get_barrier_semaphore()
    places = [{"row": lax.rem(my_row + off, count_row)} for off in sorted({1, count_row - 1})]
    places += [{"ch": lax.rem(my_ch + off, count_ch)} for off in range(1, count_ch)]
    for place in places:
        pl.semaphore_signal(barrier, inc=1, device_id=place, device_id_type=MESH)

    pl.semaphore_wait(barrier, len(places))

    part = my_ch * per
    above = pl.ds(part, per)
    below = pl.ds(margin + rows + part, per)

    def sent_down():
        return pltpu.make_async_remote_copy(
            src_ref=x_ref.at[pl.ds(rows - margin + part, per)], dst_ref=out_ref.at[above],
            send_sem=send_sem.at[0], recv_sem=recv_sem.at[0],
            device_id={"row": lax.rem(my_row + 1, count_row)}, device_id_type=MESH,
        )

    def sent_up():
        return pltpu.make_async_remote_copy(
            src_ref=x_ref.at[pl.ds(part, per)], dst_ref=out_ref.at[below],
            send_sem=send_sem.at[1], recv_sem=recv_sem.at[1],
            device_id={"row": lax.rem(my_row + count_row - 1, count_row)}, device_id_type=MESH,
        )

    def forwards(side):
        where = (above, below)[side]
        return [
            pltpu.make_async_remote_copy(
                src_ref=out_ref.at[where], dst_ref=out_ref.at[where],
                send_sem=fwd_send.at[side, off], recv_sem=fwd_recv.at[side, off],
                device_id={"ch": lax.rem(my_ch + off, count_ch)}, device_id_type=MESH,
            )
            for off in range(1, count_ch)
        ]

    for present, send in ((has_down, sent_down), (has_up, sent_up)):
        @pl.when(present)
        def _(send=send):
            send().start()

    out_ref[margin : margin + rows] = x_ref[...]

    for side, present, send in ((0, has_up, sent_down), (1, has_down, sent_up)):
        @pl.when(present)
        def _(side=side, send=send):
            send().wait_recv()
            for copy in forwards(side):
                copy.start()

        @pl.when(jnp.logical_not(present))
        def _(side=side):
            start = (0, margin + rows)[side]
            out_ref[start : start + margin] = jnp.zeros((margin,) + x_ref.shape[1:], x_ref.dtype)

    for side, present in ((0, has_up), (1, has_down)):
        @pl.when(present)
        def _(side=side):
            for copy in forwards(side):
                copy.wait()

    for present, send in ((has_down, sent_down), (has_up, sent_up)):
        @pl.when(present)
        def _(send=send):
            send().wait_send()


def halo_call(mesh, flat, margin):
    rows, span, lanes = flat.shape
    anywhere = pl.BlockSpec(memory_space=pltpu.VMEM)
    dma = pltpu.SemaphoreType.DMA
    return pl.pallas_call(
        functools.partial(halo_kernel, mesh["row"], mesh["ch"], margin),
        in_specs=[anywhere],
        out_specs=anywhere,
        out_shape=jax.ShapeDtypeStruct((rows + 2 * margin, span, lanes), flat.dtype),
        scratch_shapes=[
            dma((2,)), dma((2,)), dma((2, mesh["ch"])), dma((2, mesh["ch"])),
        ],
        compiler_params=pltpu.CompilerParams(
            collective_id=2, has_side_effects=True, vmem_limit_bytes=12 << 20
        ),
    )(flat)


def on_device(
    shape, x_center, x_gens, w_expand, b_expand, w_depth, b_depth, w_reduce, b_reduce, w_excite, b_excite
):
    gens, rows, cols, c_in = x_gens.shape
    chans = w_expand.shape[1]
    taps = w_depth.shape[0]
    margin = taps // 2
    weights = merged_weights(w_expand, b_expand, w_depth)
    ones = jnp.ones((rows, cols, 1), jnp.bfloat16)
    center = jnp.concatenate([x_center, ones], axis=-1)
    center = jnp.pad(center, ((0, 0), (0, cols), (0, LANES - c_in - 1)))
    flat = x_gens.transpose(1, 0, 2, 3).reshape(rows, gens * cols, c_in)
    flat = jnp.concatenate([jnp.pad(flat, ((0, 0), (0, 0), (0, LANES - c_in))), center], axis=1)
    x_rows = halo_call(shape, flat, margin)
    dw_gens, dw_center, local_radius, sum_gens, sum_center = conv_call(
        x_rows, weights, b_depth, gens, rows, taps, cols
    )
    gates, stats, feat = exchange_call(
        shape, local_radius, sum_gens, sum_center, w_reduce.T, b_reduce, w_excite, b_excite
    )
    return final_call(dw_gens, gates, dw_center, feat, stats)


def solution(mesh):
    in_specs = (
        P(("grp", "row"), None, None),
        P(("grp", "gen"), "row", None, None),
        P(None, "ch"),
        P("ch"),
        P(None, None, "ch"),
        P("ch"),
        P(),
        P(),
        P(None, "ch"),
        P("ch"),
    )
    out_specs = (
        P(("grp", "row"), None, "ch"),
        P(("grp", "gen"), "row", None, "ch"),
        P(("grp", "row"), None, "ch"),
    )
    return jax.shard_map(
        functools.partial(on_device, dict(mesh.shape)), mesh=mesh, in_specs=in_specs, out_specs=out_specs, check_vma=False
    )
```

```python
import functools

import jax
import jax.numpy as jnp
from jax import lax
from jax.experimental import pallas as pl
from jax.experimental.pallas import tpu as pltpu
from jax.sharding import PartitionSpec as P

MESH = pl.DeviceIdType.MESH
LANES = 128
BLOCK = 8


def conv_rows(source, w_ref, shifted_ref, acc_ref, rows, taps, cols):
    margin = taps // 2
    depth, span, lanes = source.shape
    values = source.astype(jnp.float32).reshape(depth * span, lanes)
    col = lax.broadcasted_iota(jnp.int32, (depth * span, lanes), 0) % cols
    for tap_col in range(taps):
        shift = tap_col - margin
        moved = values
        if shift != 0:
            moved = pltpu.roll(values, (-shift) % (depth * span), 0)
            keep = (col + shift >= 0) & (col + shift < cols)
            moved = jnp.where(keep, moved, 0.0)
        shifted_ref[tap_col, :, :span, :] = moved.astype(jnp.bfloat16).reshape(depth, span, lanes)
    lhs = jnp.concatenate(
        [
            shifted_ref[tap_col, tap_row : tap_row + rows, :span, :].reshape(rows * span, lanes)
            for tap_col in range(taps)
            for tap_row in range(taps)
        ],
        axis=-1,
    )
    acc_ref[: rows * span, :] = jnp.dot(lhs, w_ref[...], preferred_element_type=jnp.float32)


def conv_kernel(
    rows, taps, cols, block, chans,
    x_ref, w_ref, bd_ref,
    dwg_ref, dwc_ref, rad_ref, pg_ref, pc_ref,
    shifted_ref, acc_ref,
):
    step = pl.program_id(0)

    @pl.when(step == 0)
    def _():
        conv_rows(x_ref[:, -2 * cols :], w_ref, shifted_ref, acc_ref, rows, taps, cols)
        total = jnp.zeros((cols, chans), jnp.float32)
        for row in range(rows):
            one = acc_ref[row * 2 * cols : row * 2 * cols + cols, :chans] + bd_ref[...][None, :]
            dwc_ref[row] = one
            total = total + one
        pc_ref[...] = jnp.sum(total, axis=0, keepdims=True)
        rad_ref[...] = jnp.zeros_like(rad_ref)

    span = block * cols
    here = pl.ds(pl.multiple_of(step * span, span), span)
    conv_rows(x_ref[:, here], w_ref, shifted_ref, acc_ref, rows, taps, cols)
    totals = [jnp.zeros((cols, chans), jnp.float32) for _ in range(block)]
    for row in range(rows):
        radius = rad_ref[row]
        for k in range(block):
            start = (row * block + k) * cols
            one = acc_ref[start : start + cols, :chans].astype(jnp.bfloat16)
            dwg_ref[k, row] = one
            wide = one.astype(jnp.float32)
            radius = radius + jnp.abs(wide)
            totals[k] = totals[k] + wide
        rad_ref[row] = radius
    for k in range(block):
        pg_ref[k] = jnp.sum(totals[k], axis=0, keepdims=True)


def conv_call(x_rows, weights, b_depth, gens, rows, taps, cols):
    chans = b_depth.shape[0]
    depth = rows + taps - 1
    wide = weights.shape[-1]
    block = BLOCK
    return pl.pallas_call(
        functools.partial(conv_kernel, rows, taps, cols, block, chans),
        grid=(gens // block,),
        in_specs=[
            pl.BlockSpec(memory_space=pltpu.VMEM),
            pl.BlockSpec(memory_space=pltpu.VMEM),
            pl.BlockSpec(memory_space=pltpu.VMEM),
        ],
        out_specs=[
            pl.BlockSpec((block, rows, cols, chans), lambda i: (i, 0, 0, 0)),
            pl.BlockSpec((rows, cols, chans), lambda i: (0, 0, 0)),
            pl.BlockSpec((rows, cols, chans), lambda i: (0, 0, 0)),
            pl.BlockSpec((block, 1, chans), lambda i: (i, 0, 0)),
            pl.BlockSpec((1, chans), lambda i: (0, 0)),
        ],
        out_shape=[
            jax.ShapeDtypeStruct((gens, rows, cols, chans), jnp.bfloat16),
            jax.ShapeDtypeStruct((rows, cols, chans), jnp.float32),
            jax.ShapeDtypeStruct((rows, cols, chans), jnp.float32),
            jax.ShapeDtypeStruct((gens, 1, chans), jnp.float32),
            jax.ShapeDtypeStruct((1, chans), jnp.float32),
        ],
        scratch_shapes=[
            pltpu.VMEM((taps, depth, block * cols, LANES), jnp.bfloat16),
            pltpu.VMEM((rows * block * cols, wide), jnp.float32),
        ],
        compiler_params=pltpu.CompilerParams(
            dimension_semantics=("arbitrary",), vmem_limit_bytes=32 << 20
        ),
        cost_estimate=pl.CostEstimate(
            flops=2 * gens * rows * cols * taps * taps * LANES * wide,
            bytes_accessed=10 << 20,
            transcendentals=0,
        ),
    )(x_rows, weights, b_depth)


def relax_gate(ex_center, gate_radius):
    low_end = ex_center - gate_radius
    high_end = ex_center + gate_radius
    sig_low = jax.nn.sigmoid(low_end)
    sig_high = jax.nn.sigmoid(high_end)
    slope_val = jnp.minimum(sig_low * (1.0 - sig_low), sig_high * (1.0 - sig_high))
    gate_center = slope_val * ex_center + 0.5 * (
        sig_high + sig_low - slope_val * (high_end + low_end)
    )
    spread_term = 0.5 * (sig_high - sig_low - slope_val * (high_end - low_end))
    return (gate_center, slope_val, spread_term)


def exchange_kernel(
    gens, rows, cols, count_gen, count_row, count_ch, per,
    rad_ref, sg_ref, sc_ref, wr_ref, br_ref, we_ref, be_ref,
    gates_ref, stats_ref, feat_ref,
    send_rad, recv_rad, full_rad, squeeze, gate,
    rs_send, rs_recv, ag_send, ag_recv, sq_send, sq_recv, gt_send, gt_recv,
):
    my_gen = lax.axis_index("gen")
    my_row = lax.axis_index("row")
    my_ch = lax.axis_index("ch")
    chans = stats_ref.shape[-1]
    cells = rows * cols * count_row
    gen_peers = [(off, {"gen": lax.rem(my_gen + off, count_gen)}) for off in range(1, count_gen)]
    side_peers = []
    for off_row in range(count_row):
        for off_ch in range(count_ch):
            if off_row or off_ch:
                place = {
                    "row": lax.rem(my_row + off_row, count_row),
                    "ch": lax.rem(my_ch + off_ch, count_ch),
                }
                side_peers.append((off_row * count_ch + off_ch, place))
    barrier = pltpu.get_barrier_semaphore()
    for _, place in gen_peers + side_peers:
        pl.semaphore_signal(barrier, inc=1, device_id=place, device_id_type=MESH)

    pooled = jnp.concatenate(
        [sg_ref[...][:, 0], sc_ref[...], jnp.zeros((7, chans), jnp.float32)], axis=0
    ) * (1.0 / cells)
    own = wr_ref[:, :chans]
    for other in range(1, count_ch):
        own = jnp.where(my_ch == other, wr_ref[:, other * chans : (other + 1) * chans], own)
    part = lax.dot_general(
        pooled,
        own,
        (((1,), (1,)), ((), ())),
        precision=lax.Precision.HIGHEST,
        preferred_element_type=jnp.float32,
    )
    mine = my_row * count_ch + my_ch
    squeeze[mine] = part
    tiles = rows * cols // 8
    send_rad[:tiles] = rad_ref[...].reshape(tiles, 8, chans).astype(jnp.bfloat16)
    if count_gen * per > tiles:
        send_rad[tiles:] = jnp.zeros((count_gen * per - tiles, 8, chans), jnp.bfloat16)
    recv_rad[my_gen] = send_rad[pl.ds(my_gen * per, per)]

    pl.semaphore_wait(barrier, len(gen_peers) + len(side_peers))

    def remote(src, dst, send_sem, recv_sem, place):
        return pltpu.make_async_remote_copy(
            src_ref=src, dst_ref=dst, send_sem=send_sem, recv_sem=recv_sem,
            device_id=place, device_id_type=MESH,
        )

    sq_copies = [
        remote(squeeze.at[mine], squeeze.at[mine], sq_send.at[off], sq_recv.at[off], place)
        for off, place in side_peers
    ]
    rs_copies = [
        remote(
            send_rad.at[pl.ds(place["gen"] * per, per)], recv_rad.at[my_gen],
            rs_send.at[off], rs_recv.at[off], place,
        )
        for off, place in gen_peers
    ]
    for copy in sq_copies + rs_copies:
        copy.start()
    for copy in sq_copies:
        copy.wait()
    total = squeeze[0]
    for slot in range(1, count_row * count_ch):
        total = total + squeeze[slot]
    row_of = lax.broadcasted_iota(jnp.int32, total.shape, 0)
    total = total + jnp.where(row_of == gens, br_ref[...][None, :], 0.0)
    ex_all = jnp.dot(
        total, we_ref[...], precision=lax.Precision.HIGHEST, preferred_element_type=jnp.float32
    )
    ex_gens = ex_all[:gens]
    ex_center = ex_all[gens : gens + 1] + be_ref[...][None, :]
    gate[my_gen] = jnp.sum(jnp.abs(ex_gens), axis=0, keepdims=True)
    gt_copies = [
        remote(gate.at[my_gen], gate.at[my_gen], gt_send.at[off], gt_recv.at[off], place)
        for off, place in gen_peers
    ]
    for copy in gt_copies:
        copy.start()

    for copy in rs_copies:
        copy.wait()
    chunk = recv_rad[0].astype(jnp.float32)
    for slot in range(1, count_gen):
        chunk = chunk + recv_rad[slot].astype(jnp.float32)
    own = pl.ds(my_gen * per, per)
    full_rad[own] = chunk.astype(jnp.bfloat16)
    ag_copies = [
        remote(full_rad.at[own], full_rad.at[own], ag_send.at[off], ag_recv.at[off], place)
        for off, place in gen_peers
    ]
    for copy in ag_copies:
        copy.start()

    for copy in gt_copies:
        copy.wait()
    gate_radius = gate[0]
    for slot in range(1, count_gen):
        gate_radius = gate_radius + gate[slot]
    gate_center, slope_val, spread_term = relax_gate(ex_center, gate_radius)
    gates_ref[...] = (slope_val * ex_gens)[:, None, :]
    gate_total = slope_val * gate_radius + spread_term
    stats_ref[0:1] = gate_center
    stats_ref[1:2] = spread_term
    stats_ref[2:3] = gate_total
    for copy in ag_copies:
        copy.wait()
    feat_ref[...] = full_rad[:tiles].astype(jnp.float32).reshape(rows, cols, chans)


def exchange_call(mesh, radius, sum_gens, sum_center, w_reduce, b_reduce, w_excite, b_excite):
    rows, cols, chans = radius.shape
    gens = sum_gens.shape[0]
    count_gen, count_row, count_ch = mesh["gen"], mesh["row"], mesh["ch"]
    per = -(-(rows * cols // 8) // count_gen)
    units = w_excite.shape[0]
    vmem = pl.BlockSpec(memory_space=pltpu.VMEM)
    side = count_row * count_ch
    dma = pltpu.SemaphoreType.DMA
    return pl.pallas_call(
        functools.partial(exchange_kernel, gens, rows, cols, count_gen, count_row, count_ch, per),
        in_specs=[vmem] * 7,
        out_specs=[vmem] * 3,
        out_shape=[
            jax.ShapeDtypeStruct((gens, 1, chans), jnp.float32),
            jax.ShapeDtypeStruct((3, chans), jnp.float32),
            jax.ShapeDtypeStruct((rows, cols, chans), jnp.float32),
        ],
        scratch_shapes=[
            pltpu.VMEM((count_gen * per, 8, chans), jnp.bfloat16),
            pltpu.VMEM((count_gen, per, 8, chans), jnp.bfloat16),
            pltpu.VMEM((count_gen * per, 8, chans), jnp.bfloat16),
            pltpu.VMEM((side, gens + 8, units), jnp.float32),
            pltpu.VMEM((count_gen, 1, chans), jnp.float32),
            dma((count_gen,)), dma((count_gen,)), dma((count_gen,)), dma((count_gen,)),
            dma((side,)), dma((side,)), dma((count_gen,)), dma((count_gen,)),
        ],
        compiler_params=pltpu.CompilerParams(
            collective_id=1, has_side_effects=True, vmem_limit_bytes=12 << 20
        ),
    )(radius, sum_gens, sum_center, w_reduce, b_reduce, w_excite, b_excite)


def final_kernel(block, dwg_ref, gates_ref, dwc_ref, feat_ref, stats_ref, oc_ref, og_ref, ob_ref):
    center = dwc_ref[...]
    gate_center = stats_ref[0:1]

    @pl.when(pl.program_id(0) == 0)
    def _():
        oc_ref[...] = center * gate_center
        ob_ref[...] = jnp.abs(center) * stats_ref[1:2] + feat_ref[...] * stats_ref[2:3]

    for k in range(block):
        og_ref[k] = (
            center * gates_ref[k] + gate_center * dwg_ref[k].astype(jnp.float32)
        ).astype(jnp.bfloat16)


def final_call(dw_gens, gates, dw_center, feat, stats):
    gens, rows, cols, chans = dw_gens.shape
    block = 4
    whole = pl.BlockSpec((rows, cols, chans), lambda i: (0, 0, 0))
    big = pl.BlockSpec((block, rows, cols, chans), lambda i: (i, 0, 0, 0))
    return pl.pallas_call(
        functools.partial(final_kernel, block),
        grid=(gens // block,),
        in_specs=[
            big,
            pl.BlockSpec((block, 1, chans), lambda i: (i, 0, 0)),
            whole,
            whole,
            pl.BlockSpec((3, chans), lambda i: (0, 0)),
        ],
        out_specs=[whole, big, whole],
        out_shape=[
            jax.ShapeDtypeStruct((rows, cols, chans), jnp.float32),
            jax.ShapeDtypeStruct(dw_gens.shape, jnp.bfloat16),
            jax.ShapeDtypeStruct((rows, cols, chans), jnp.float32),
        ],
        compiler_params=pltpu.CompilerParams(
            dimension_semantics=("arbitrary",), vmem_limit_bytes=12 << 20
        ),
    )(dw_gens, gates, dw_center, feat, stats)


def merged_weights(w_expand, b_expand, w_depth):
    taps = w_depth.shape[0]
    c_in, chans = w_expand.shape
    wide = -(-chans // LANES) * LANES
    mixed = jnp.concatenate([w_expand.astype(jnp.float32), b_expand[None]], axis=0)
    mixed = jnp.pad(mixed, ((0, LANES - c_in - 1), (0, wide - chans)))
    depth = jnp.pad(w_depth, ((0, 0), (0, 0), (0, wide - chans))).transpose(1, 0, 2)
    merged = (depth[:, :, None, :] * mixed[None, None]).astype(jnp.bfloat16)
    return merged.reshape(taps * taps * LANES, wide)


def halo_kernel(count_row, count_ch, margin, x_ref, out_ref, send_sem, recv_sem, fwd_send, fwd_recv):
    rows = x_ref.shape[0]
    per = margin // count_ch
    my_row = lax.axis_index("row")
    my_ch = lax.axis_index("ch")
    has_up = my_row > 0
    has_down = my_row < count_row - 1
    barrier = pltpu.get_barrier_semaphore()
    places = [{"row": lax.rem(my_row + off, count_row)} for off in sorted({1, count_row - 1})]
    places += [{"ch": lax.rem(my_ch + off, count_ch)} for off in range(1, count_ch)]
    for place in places:
        pl.semaphore_signal(barrier, inc=1, device_id=place, device_id_type=MESH)

    pl.semaphore_wait(barrier, len(places))

    part = my_ch * per
    above = pl.ds(part, per)
    below = pl.ds(margin + rows + part, per)

    def sent_down():
        return pltpu.make_async_remote_copy(
            src_ref=x_ref.at[pl.ds(rows - margin + part, per)], dst_ref=out_ref.at[above],
            send_sem=send_sem.at[0], recv_sem=recv_sem.at[0],
            device_id={"row": lax.rem(my_row + 1, count_row)}, device_id_type=MESH,
        )

    def sent_up():
        return pltpu.make_async_remote_copy(
            src_ref=x_ref.at[pl.ds(part, per)], dst_ref=out_ref.at[below],
            send_sem=send_sem.at[1], recv_sem=recv_sem.at[1],
            device_id={"row": lax.rem(my_row + count_row - 1, count_row)}, device_id_type=MESH,
        )

    def forwards(side):
        where = (above, below)[side]
        return [
            pltpu.make_async_remote_copy(
                src_ref=out_ref.at[where], dst_ref=out_ref.at[where],
                send_sem=fwd_send.at[side, off], recv_sem=fwd_recv.at[side, off],
                device_id={"ch": lax.rem(my_ch + off, count_ch)}, device_id_type=MESH,
            )
            for off in range(1, count_ch)
        ]

    for present, send in ((has_down, sent_down), (has_up, sent_up)):
        @pl.when(present)
        def _(send=send):
            send().start()

    out_ref[margin : margin + rows] = x_ref[...]

    for side, present, send in ((0, has_up, sent_down), (1, has_down, sent_up)):
        @pl.when(present)
        def _(side=side, send=send):
            send().wait_recv()
            for copy in forwards(side):
                copy.start()

        @pl.when(jnp.logical_not(present))
        def _(side=side):
            start = (0, margin + rows)[side]
            out_ref[start : start + margin] = jnp.zeros((margin,) + x_ref.shape[1:], x_ref.dtype)

    for side, present in ((0, has_up), (1, has_down)):
        @pl.when(present)
        def _(side=side):
            for copy in forwards(side):
                copy.wait()

    for present, send in ((has_down, sent_down), (has_up, sent_up)):
        @pl.when(present)
        def _(send=send):
            send().wait_send()


def halo_call(mesh, flat, margin):
    rows, span, lanes = flat.shape
    anywhere = pl.BlockSpec(memory_space=pltpu.VMEM)
    dma = pltpu.SemaphoreType.DMA
    return pl.pallas_call(
        functools.partial(halo_kernel, mesh["row"], mesh["ch"], margin),
        in_specs=[anywhere],
        out_specs=anywhere,
        out_shape=jax.ShapeDtypeStruct((rows + 2 * margin, span, lanes), flat.dtype),
        scratch_shapes=[
            dma((2,)), dma((2,)), dma((2, mesh["ch"])), dma((2, mesh["ch"])),
        ],
        compiler_params=pltpu.CompilerParams(
            collective_id=2, has_side_effects=True, vmem_limit_bytes=12 << 20
        ),
    )(flat)


def on_device(
    shape, x_center, x_gens, w_expand, b_expand, w_depth, b_depth, w_reduce, b_reduce, w_excite, b_excite
):
    gens, rows, cols, c_in = x_gens.shape
    chans = w_expand.shape[1]
    taps = w_depth.shape[0]
    margin = taps // 2
    weights = merged_weights(w_expand, b_expand, w_depth)
    ones = jnp.ones((rows, cols, 1), jnp.bfloat16)
    center = jnp.concatenate([x_center, ones], axis=-1)
    center = jnp.pad(center, ((0, 0), (0, cols), (0, LANES - c_in - 1)))
    flat = x_gens.transpose(1, 0, 2, 3).reshape(rows, gens * cols, c_in)
    flat = jnp.concatenate([jnp.pad(flat, ((0, 0), (0, 0), (0, LANES - c_in))), center], axis=1)
    x_rows = halo_call(shape, flat, margin)
    dw_gens, dw_center, local_radius, sum_gens, sum_center = conv_call(
        x_rows, weights, b_depth, gens, rows, taps, cols
    )
    gates, stats, feat = exchange_call(
        shape, local_radius, sum_gens, sum_center, w_reduce.T, b_reduce, w_excite, b_excite
    )
    return final_call(dw_gens, gates, dw_center, feat, stats)


def solution(mesh):
    in_specs = (
        P(("grp", "row"), None, None),
        P(("grp", "gen"), "row", None, None),
        P(None, "ch"),
        P("ch"),
        P(None, None, "ch"),
        P("ch"),
        P(),
        P(),
        P(None, "ch"),
        P("ch"),
    )
    out_specs = (
        P(("grp", "row"), None, "ch"),
        P(("grp", "gen"), "row", None, "ch"),
        P(("grp", "row"), None, "ch"),
    )
    return jax.shard_map(
        functools.partial(on_device, dict(mesh.shape)), mesh=mesh, in_specs=in_specs, out_specs=out_specs, check_vma=False
    )
```
